128 devices in a mesh: row: 16 (over z, y), ga: 8 (over x, core).
Axes of the slice: x: 4, y: 4, z: 4, core: 2. Of those that a mesh axis runs over, the one named last changes fastest.
Arguments:
- fine_feats: bfloat16 [15360, 64, 512], P(('row', 'ga')), may hold values from -6 to 6
- fine_child: int32 [15360], P(('row', 'ga')), may hold values from -1 to 511, as said below
- parent_block: int32 [1024], P(('row', 'ga')), may hold values from 0 to 63, as said below
- w_parent: bfloat16 [64, 128], replicated, may hold values from -2 to 2
- w_root_in: bfloat16 [128, 256], replicated, may hold values from -1.5 to 1.5
- w_root: bfloat16 [256, 256, 3, 3, 3], P('ga'), may hold values from -0.15625 to 0.15625
- root_bias: float32 [256], P('ga'), may hold values from -0.5 to 0.5
- w_down: bfloat16 [256, 128], replicated, may hold values from -0.375 to 0.375
- w_skip: bfloat16 [128, 64], replicated, may hold values from -0.5 to 0.5
Outputs:
- fine_out: bfloat16 [15360, 64, 512], P(('row', 'ga'))
- root_features: bfloat16 [256, 64, 32, 32], P('ga', 'row')
The draws below stay inside these ranges and needn't reach their ends.
Inputs may be any that keep to these rules, and one draw needn't show every extreme that they name: `fine_child`: parents i * 8 to (i + 1) * 8 - 1 of a region belong to the region's device of ga index i. Over the slots of a region every child index 0 to 511 appears exactly once. The slots of one device hold at most 15 children of one device's parents, and in every region some device holds exactly 15 children of each device's parents. `parent_block`: the parents of one region have distinct places.
All inputs are finite; a program needn't handle non-finite values.
Results may differ from the reference program's by a relative error of at most 0.013.
Values may be sent and summed in bfloat16 or wider, within the bound.
A program may use at most 128 MiB of HBM per device.

```python
import jax
import jax.numpy as jnp
from jax import lax

C1 = 64
C2 = 128
C3 = 256
B = 8
PAR_DEV = 8
RXY = 32
RZ_REG = 4
PARENTS = 1024
FINE_DEV = 120
FINE_SLOTS = 15360
RZ = 64
N_ROW = 16
N_GA = 8


def draw_region_children(region_key):
    groups = N_GA
    child_quota = 8 * PAR_DEV
    unit_load = child_quota // (groups * groups)
    split_keys = jax.random.split(region_key, 3)
    load_order = jax.random.permutation(split_keys[0], groups)
    send_loads = (2 * load_order + 1) * unit_load
    starts = jnp.cumsum(send_loads) - send_loads

    def shuffle_children(subkey):
        return jax.random.permutation(subkey, child_quota)

    def shuffle_slots(subkey):
        return jax.random.permutation(subkey, FINE_DEV)
    positions = jax.vmap(shuffle_children)(jax.random.split(split_keys[1], groups))
    sender = jnp.sum((positions[:, :, None] >= starts[None, None, :]).astype(jnp.int32), axis=2) - 1
    sender = sender.reshape(-1)
    sender_hot = (sender[:, None] == jnp.arange(groups, dtype=jnp.int32)[None, :]).astype(jnp.int32)
    slot_rank = jnp.sum(jnp.cumsum(sender_hot, axis=0) * sender_hot, axis=1) - 1
    slot_orders = jax.vmap(shuffle_slots)(jax.random.split(split_keys[2], groups))
    slot_place = slot_orders[sender, slot_rank]
    filled = jnp.full((groups, FINE_DEV), -1, jnp.int32)
    return filled.at[sender, slot_place].set(jnp.arange(groups * child_quota, dtype=jnp.int32))


def draw_fine_child(key, part):
    region_keys = jax.random.split(jax.random.fold_in(key, 11), N_ROW)
    return jax.vmap(draw_region_children)(region_keys).reshape(-1).astype(jnp.int32)


def draw_parent_block(key, part):
    half_edge = B // 2
    block_total = RZ_REG // half_edge * (RXY // half_edge) ** 2

    def region_places(subkey):
        return jax.random.permutation(subkey, block_total)[:N_GA * PAR_DEV]
    region_keys = jax.random.split(jax.random.fold_in(key, 23), N_ROW)
    return jax.vmap(region_places)(region_keys).reshape(-1).astype(jnp.int32)


def levels(key, dims, shards, low, largest):
    loudness, own = 1.0, jax.random.fold_in(key, 6)
    for axis_at, parts in shards:
        draws = jnp.exp(jax.random.uniform(jax.random.fold_in(own, axis_at), (parts,), jnp.float32, low / len(shards), largest / len(shards)))
        loudness = loudness * jnp.repeat(draws, dims[axis_at] // parts).reshape([-1 if axis == axis_at else 1 for axis in range(len(dims))])
    return loudness


def scatter_about(rng, shape, scale, limit, cuts=(), held_as=jnp.bfloat16):
    values = scale * jax.random.normal(rng, shape, jnp.float32)
    if cuts:
        values = values * levels(rng, shape, cuts, -0.22, 0.18)
    return jnp.clip(values, -limit, limit).astype(held_as)


def setup_inputs(seed: int = 0) -> dict:
    seeds = jax.random.split(jax.random.key(seed), 10)
    return {
        "fine_feats": scatter_about(seeds[0], (FINE_SLOTS, C1, B ** 3), 1.0, 6.0, ((0, 128),)),
        "fine_child": draw_fine_child(jax.random.fold_in(seeds[9], 71), 0),
        "parent_block": draw_parent_block(jax.random.fold_in(seeds[9], 71), 0),
        "w_parent": scatter_about(seeds[3], (C1, C2), (C1 // 8) ** -0.5, 2.0),
        "w_root_in": scatter_about(seeds[4], (C2, C3), (C2 // 8) ** -0.5, 1.5),
        "w_root": scatter_about(seeds[5], (C3, C3, 3, 3, 3), (27 * C3 // 4) ** -0.5, 0.15625, ((0, 8),)),
        "root_bias": jnp.clip(jax.random.uniform(seeds[6], (C3,), jnp.float32, -0.5, 0.5) * levels(seeds[6], (C3,), ((0, 8),), -0.4, 0.0), -0.5, 0.5),
        "w_down": scatter_about(seeds[7], (C3, C2), C3 ** -0.5, 0.375),
        "w_skip": scatter_about(seeds[8], (C2, C1), C2 ** -0.5, 0.5),
    }


def pool_pairs(values, half_edge):
    row_count, channel_count, voxel_count = values.shape
    cube = values.astype(jnp.float32).reshape(row_count, channel_count, half_edge, 2, half_edge, 2, half_edge, 2)
    return jnp.mean(cube, axis=(3, 5, 7)).reshape(row_count, channel_count, half_edge ** 3)


def upsample_pairs(values, half_edge):
    row_count, channel_count, voxel_count = values.shape
    cube = values.reshape(row_count, channel_count, half_edge, 1, half_edge, 1, half_edge, 1)
    cube = jnp.broadcast_to(cube, (row_count, channel_count, half_edge, 2, half_edge, 2, half_edge, 2))
    return cube.reshape(row_count, channel_count, 8 * voxel_count)


def join_octants(octants, half_edge):
    parent_count = octants.shape[0]
    channel_count = octants.shape[2]
    cube = octants.reshape(parent_count, 2, 2, 2, channel_count, half_edge, half_edge, half_edge)
    cube = cube.transpose(0, 4, 1, 5, 2, 6, 3, 7)
    return cube.reshape(parent_count, channel_count, 8 * half_edge ** 3)


def split_octants(bricks, half_edge):
    parent_count = bricks.shape[0]
    channel_count = bricks.shape[1]
    cube = bricks.reshape(parent_count, channel_count, 2, half_edge, 2, half_edge, 2, half_edge)
    cube = cube.transpose(0, 2, 4, 6, 1, 3, 5, 7)
    return cube.reshape(parent_count, 8, channel_count, half_edge ** 3)


def contract(values, weights):
    return jnp.einsum("pcv,cd->pdv", values.astype(jnp.float32), weights.astype(jnp.float32), precision=lax.Precision.HIGHEST)


def contract_octants(values, weights):
    return jnp.einsum("pocv,cd->podv", values.astype(jnp.float32), weights.astype(jnp.float32), precision=lax.Precision.HIGHEST)


def reference(fine_feats, fine_child, parent_block, w_parent, w_root_in, w_root, root_bias, w_down, w_skip):
    half_edge = B // 2
    octant_voxels = half_edge ** 3
    region_total = 8 * PAR_DEV * N_GA
    slot_region = (jnp.arange(FINE_SLOTS) // (FINE_DEV * N_GA)).astype(jnp.int32)
    live_slot = fine_child >= 0
    child_index = jnp.where(live_slot, slot_region * region_total + fine_child, 8 * PARENTS).astype(jnp.int32)
    pooled = pool_pairs(fine_feats, half_edge).astype(jnp.bfloat16)
    octant_table = jnp.zeros((8 * PARENTS + 1, C1, octant_voxels), jnp.bfloat16).at[child_index].set(pooled)[:-1]
    bricks = join_octants(octant_table.reshape(PARENTS, 8, C1, octant_voxels), half_edge)
    parent_hidden = jax.nn.relu(contract(bricks, w_parent)).astype(jnp.bfloat16)
    parent_pool = pool_pairs(parent_hidden, half_edge).astype(jnp.bfloat16)
    root_input = contract(parent_pool, w_root_in).astype(jnp.bfloat16)
    block_side = RXY // half_edge
    block_layers = RZ_REG // half_edge
    block_total = block_layers * block_side * block_side
    parent_region = (jnp.arange(PARENTS) // (PAR_DEV * N_GA)).astype(jnp.int32)
    block_index = (parent_region * block_total + parent_block).astype(jnp.int32)
    placed = jnp.zeros((N_ROW * block_total, C3, octant_voxels), jnp.bfloat16).at[block_index].set(root_input)
    root_grid = placed.reshape(N_ROW, block_layers, block_side, block_side, C3, half_edge, half_edge, half_edge)
    root_grid = root_grid.transpose(4, 0, 1, 5, 2, 6, 3, 7).reshape(C3, RZ, RXY, RXY)
    convolved = lax.conv_general_dilated(root_grid[None].astype(jnp.float32), w_root.astype(jnp.float32), (1, 1, 1), ((1, 1), (1, 1), (1, 1)), dimension_numbers=("NCDHW", "OIDHW", "NCDHW"), precision=lax.Precision.HIGHEST)[0]
    root_features = jax.nn.relu(convolved + root_bias[:, None, None, None]).astype(jnp.bfloat16)
    blocks_back = root_features.reshape(C3, N_ROW, block_layers, half_edge, block_side, half_edge, block_side, half_edge)
    blocks_back = blocks_back.transpose(1, 2, 4, 6, 0, 3, 5, 7).reshape(N_ROW * block_total, C3, octant_voxels)
    parent_root = blocks_back[block_index]
    lifted = contract(parent_root, w_down)
    parent_decoded = jax.nn.relu(parent_hidden.astype(jnp.float32) + upsample_pairs(lifted, half_edge)).astype(jnp.bfloat16)
    skip_octants = contract_octants(split_octants(parent_decoded, half_edge), w_skip).astype(jnp.bfloat16)
    skip_octants = skip_octants.reshape(8 * PARENTS, C1, octant_voxels)
    fine_skip = jnp.where(live_slot[:, None, None], skip_octants[jnp.minimum(child_index, 8 * PARENTS - 1)], 0).astype(jnp.float32)
    fine_out = (fine_feats.astype(jnp.float32) + upsample_pairs(fine_skip, half_edge)).astype(jnp.bfloat16)
    return fine_out, root_features
```

```python
import functools

import jax
import jax.numpy as jnp
from jax import lax
from jax.experimental import pallas as pl
from jax.experimental.pallas import tpu as pltpu
from jax.sharding import PartitionSpec as P

BF = jnp.bfloat16
F32 = jnp.float32
I32 = jnp.int32
MESH = pl.DeviceIdType.MESH
SLOTS = 120
NB = 4
SB = 32
TB = 24


def iota(shape, dim):
    return lax.broadcasted_iota(I32, shape, dim)


def column_of(v):
    z, y, x = v >> 6, (v >> 3) & 7, v & 7
    w = (z >> 2) * 4 + (y >> 2) * 2 + (x >> 2)
    g = ((z >> 1) & 1) * 4 + ((y >> 1) & 1) * 2 + ((x >> 1) & 1)
    return g * 8 + w


def nt(a, b):
    return lax.dot_general(a, b, (((1,), (1,)), ((), ())), preferred_element_type=F32)


def tn(a, b):
    return lax.dot_general(a, b, (((0,), (0,)), ((), ())), preferred_element_type=F32)


def mm(a, b):
    return jnp.dot(a, b, preferred_element_type=F32)


def root_kernel(
    rows,
    child_ref,
    block_ref,
    x_hbm,
    wp_ref,
    win_ref,
    wc_ref,
    bias_ref,
    hid_hbm,
    back_hbm,
    nat_ref,
    xbuf,
    p8,
    hid,
    pp,
    ints,
    gathered,
    place,
    slab,
    halo,
    xt,
    taps,
    rft,
    quad,
    perm,
    msgs,
    x_sem,
    hid_sem,
    int_send,
    int_recv,
    ag_send,
    ag_recv,
    fw_send,
    fw_recv,
    halo_send,
    halo_recv,
    back_send,
    back_recv,
    own_sem,
):
    row = lax.axis_index("row")
    me = lax.axis_index("ga")
    chip = me // 2
    core = lax.rem(me, 2)
    partner = 2 * chip + 1 - core
    last = rows - 1

    def peer(k):
        return lax.rem(me + k, 8)

    def chip_peer(k):
        return 2 * lax.rem(chip + k, 4) + core

    def at(ga):
        return (row, ga)

    x_copies = []
    for blk in range(NB):
        n = min(SB, SLOTS - blk * SB)
        x_copies.append(
            pltpu.make_async_copy(
                x_hbm.at[pl.ds(blk * SB, n)], xbuf.at[blk, pl.ds(0, n)], x_sem.at[blk]
            )
        )
        x_copies[-1].start()
    tail = SLOTS - (NB - 1) * SB
    xbuf[NB - 1, tail:] = jnp.zeros((SB - tail, 64, 512), BF)

    barrier = pltpu.get_barrier_semaphore()
    for k in range(1, 8):
        pl.semaphore_signal(barrier, inc=1, device_id=at(peer(k)), device_id_type=MESH)

    @pl.when(row > 0)
    def _():
        pl.semaphore_signal(barrier, inc=1, device_id=(row - 1, me), device_id_type=MESH)

    @pl.when(row < last)
    def _():
        pl.semaphore_signal(barrier, inc=1, device_id=(row + 1, me), device_id_type=MESH)

    ints[me] = jnp.full((8, 128), -1, I32)
    ints[me, 0:1, 0:SLOTS] = child_ref[...]
    ints[me, 1:2, 0:8] = block_ref[...]
    where = column_of(iota((512, 256), 0))
    lane = iota((512, 256), 1)
    for k in range(4):
        p8[k] = jnp.where(lane == where + 64 * k, 0.125, 0.0).astype(BF)

    sides = (row > 0).astype(I32) + (row < last).astype(I32)
    pl.semaphore_wait(barrier, 7 + sides)

    int_copies = []
    for k in range(1, 8):
        int_copies.append(
            pltpu.make_async_remote_copy(
                ints.at[me],
                ints.at[me],
                int_send.at[k],
                int_recv.at[k],
                device_id=at(peer(k)),
                device_id_type=MESH,
            )
        )
        int_copies[-1].start()

    def piece(ga, blk):
        return gathered.at[pl.ds(pl.multiple_of(ga * 128 + blk * SB, SB), SB)]

    hid_copies, ag_copies, fw_copies = [], [], []
    for blk in range(NB):
        x_copies[blk].wait()
        pooled = None
        for k in range(4):
            x = jnp.concatenate([xbuf[blk, 4 * g + k] for g in range(SB // 4)], axis=0)
            part = mm(x, p8[k])
            pooled = part if pooled is None else pooled + part
        pooled = pooled.astype(BF)
        for g in range(SB // 4):
            h = tn(pooled[g * 64 : (g + 1) * 64], wp_ref[...])
            h = jnp.maximum(h, 0.0).astype(BF)
            hid[pl.ds((blk * SB + 4 * g) * 64, 256), :] = h
            mean = jnp.sum(h.astype(F32).reshape(4, 8, 8, 128), axis=1) * 0.125
            pp[pl.ds(g * 32, 32), :] = mean.reshape(32, 128)
        start = pl.multiple_of(me * 128 + blk * SB, SB)
        for w in range(8):
            gathered[pl.ds(start, SB), w * 128 : (w + 1) * 128] = pp[
                pl.ds(w, SB, stride=8), :
            ].astype(BF)
        n = min(SB, SLOTS - blk * SB)
        hid_copies.append(
            pltpu.make_async_copy(
                hid.at[pl.ds(blk * SB * 64, n * 64)],
                hid_hbm.at[pl.ds(blk * SB * 64, n * 64)],
                hid_sem.at[blk],
            )
        )
        hid_copies[-1].start()
        for k in (2, 1, 3):
            ag_copies.append(
                pltpu.make_async_remote_copy(
                    piece(me, blk),
                    piece(me, blk),
                    ag_send.at[blk, k],
                    ag_recv.at[blk, k],
                    device_id=at(chip_peer(k)),
                    device_id_type=MESH,
                )
            )
            ag_copies[-1].start()
        fw_copies.append(
            pltpu.make_async_remote_copy(
                piece(me, blk),
                piece(me, blk),
                fw_send.at[blk, 0],
                fw_recv.at[blk, 0],
                device_id=at(partner),
                device_id_type=MESH,
            )
        )
        fw_copies[-1].start()

    for k in range(1, 8):
        int_copies[k - 1].wait()
    child = jnp.concatenate([ints[m, 0:1, :] for m in range(8)], axis=0)
    parent = child >> 3
    block = jnp.zeros((8, 128), I32)
    for m in range(8):
        blocks = ints[m, 1:2, :]
        for i in range(8):
            block = jnp.where(parent == 8 * m + i, blocks[:, i : i + 1], block)
    octant = child & 7
    pos = (
        (octant >> 2) * 256
        + (2 * (block >> 3) + ((octant >> 1) & 1)) * 16
        + 2 * (block & 7)
        + (octant & 1)
    )
    pos = jnp.where(child >= 0, pos, -1)
    for m in range(8):
        hot = iota((512, 128), 0) == pos[m : m + 1, :]
        place[:, m * 128 : (m + 1) * 128] = jnp.where(hot, 1.0, 0.0).astype(BF)
    for c in range(4):
        p = iota((1024, 256), 0)
        q = iota((1024, 256), 1) + 256 * c
        iy, ix, oy, ox = p >> 9, (p >> 8) & 1, (p >> 4) & 15, p & 15
        hot = q == (2 * oy + iy) * 32 + 2 * ox + ix
        perm[:, c * 256 : (c + 1) * 256] = jnp.where(hot, 1.0, 0.0).astype(BF)

    for blk in range(NB):
        for k in (1, 3, 2):
            src = chip_peer(4 - k)
            pltpu.make_async_remote_copy(
                piece(me, blk),
                piece(src, blk),
                ag_send.at[blk, k],
                ag_recv.at[blk, k],
                device_id=at(partner),
                device_id_type=MESH,
            ).wait_recv()
            fw_copies.append(
                pltpu.make_async_remote_copy(
                    piece(src, blk),
                    piece(src, blk),
                    fw_send.at[blk, k],
                    fw_recv.at[blk, k],
                    device_id=at(partner),
                    device_id_type=MESH,
                )
            )
            fw_copies[-1].start()
    for c in fw_copies:
        c.wait_recv()

    for i in range(4):
        slab[:, i * 256 : (i + 1) * 256] = mm(
            place[...], gathered[:, i * 256 : (i + 1) * 256]
        ).astype(BF)

    low = pltpu.make_async_remote_copy(
        slab.at[pl.ds(0, 256), pl.ds(0, 512)],
        halo.at[1],
        halo_send.at[0],
        halo_recv.at[1],
        device_id=(jnp.maximum(row - 1, 0), me),
        device_id_type=MESH,
    )
    high = pltpu.make_async_remote_copy(
        slab.at[pl.ds(256, 256), pl.ds(512, 512)],
        halo.at[0],
        halo_send.at[1],
        halo_recv.at[0],
        device_id=(jnp.minimum(row + 1, last), me),
        device_id_type=MESH,
    )

    @pl.when(row > 0)
    def _():
        low.start()

    @pl.when(row < last)
    def _():
        high.start()

    win = win_ref[...]
    for w in range(8):
        r = mm(slab[:, w * 128 : (w + 1) * 128], win).astype(BF)
        for oz in range(2):
            xt[1 + 2 * oz + (w >> 2), w & 3] = r[oz * 256 : (oz + 1) * 256]

    spot = iota((32, 256), 1)
    oy, ox = spot >> 4, spot & 15
    bias = jnp.sum(
        jnp.where(iota((32, 32), 0) == iota((32, 32), 1), bias_ref[...], 0.0),
        axis=1,
        keepdims=True,
    )

    def convolve(z):
        for ab in range(4):
            acc = None
            for dz in range(3):
                part = nt(wc_ref[dz * 288 : (dz + 1) * 288], xt[z + dz, ab])
                acc = part if acc is None else acc + part
            taps[ab] = acc

        def tap(a, b, dy, dx):
            t = ((dy + 1) * 3 + dx + 1) * 32
            return taps[2 * a + b, t : t + 32, :]

        for iy in range(2):
            for ix in range(2):
                ys = [(iy, 0), (1 - iy, 1 - 2 * iy)]
                xs = [(ix, 0), (1 - ix, 1 - 2 * ix)]
                ysh = (1 - iy, 2 * iy - 1)
                xsh = (1 - ix, 2 * ix - 1)
                by, bx = (15, 15)
                plain = sum(tap(a, b, dy, dx) for a, dy in ys for b, dx in xs)
                only_x = sum(tap(a, xsh[0], dy, xsh[1]) for a, dy in ys)
                only_y = sum(tap(ysh[0], b, ysh[1], dx) for b, dx in xs)
                both = tap(ysh[0], xsh[0], ysh[1], xsh[1])

                def shift_x(v):
                    v = pltpu.roll(v, 255 if ix else 1, 1)
                    return jnp.where(ox == (bx if ix else 0), 0.0, v)

                def shift_y(v):
                    v = pltpu.roll(v, 240 if iy else 16, 1)
                    return jnp.where(oy == (by if iy else 0), 0.0, v)

                total = plain + shift_x(only_x) + shift_y(only_y + shift_x(both))
                out = jnp.maximum(total + bias, 0.0).astype(BF)
                w = (z & 1) * 4 + iy * 2 + ix
                rft[w * 32 : (w + 1) * 32, (z >> 1) * 256 : ((z >> 1) + 1) * 256] = out
                c = iy * 2 + ix
                quad[z * 32 : (z + 1) * 32, c * 256 : (c + 1) * 256] = out

    convolve(1)
    convolve(2)

    @pl.when(row > 0)
    def _():
        high.wait_recv()

    @pl.when(row < last)
    def _():
        low.wait_recv()

    @pl.when(row == 0)
    def _():
        halo[0] = jnp.zeros((256, 512), BF)

    @pl.when(row == last)
    def _():
        halo[1] = jnp.zeros((256, 512), BF)

    for side in range(2):
        for c in range(4):
            xt[5 * side, c] = mm(halo[side, :, c * 128 : (c + 1) * 128], win).astype(BF)
    convolve(0)
    convolve(3)

    for i in range(4):
        m2 = mm(rft[...], place[:, i * 256 : (i + 1) * 256]).astype(BF)
        msgs[2 * i] = m2[:, :128]
        msgs[2 * i + 1] = m2[:, 128:]
    back_copies = []
    for k in (4, 3, 5, 2, 6, 1, 7):
        back_copies.append(
            pltpu.make_async_remote_copy(
                msgs.at[peer(k)],
                back_hbm.at[me],
                back_send.at[k],
                back_recv.at[k],
                device_id=at(peer(k)),
                device_id_type=MESH,
            )
        )
        back_copies[-1].start()
    own = pltpu.make_async_copy(msgs.at[me], back_hbm.at[me], own_sem)
    own.start()

    for i in range(4):
        n4 = mm(quad[...], perm[:, i * 256 : (i + 1) * 256]).astype(BF)
        for z in range(4):
            nat_ref[z, :, i * 256 : (i + 1) * 256] = n4[z * 32 : (z + 1) * 32]

    for c in hid_copies:
        c.wait()
    for c in ag_copies:
        c.wait_send()
    for c in fw_copies:
        c.wait_send()

    @pl.when(row > 0)
    def _():
        low.wait_send()

    @pl.when(row < last)
    def _():
        high.wait_send()

    own.wait()
    for c in back_copies:
        c.wait()


def fine_kernel(child_ref, x_ref, hid_ref, back_ref, wd_ref, ws_ref, out_ref, up, lifted):
    step = pl.program_id(0)

    @pl.when(step == 0)
    def _():
        where = column_of(iota((256, 512), 1))
        line = iota((256, 512), 0)
        for k in range(4):
            up[k] = jnp.where(line == where + 64 * k, 1.0, 0.0).astype(BF)
        for w in range(8):
            r = jnp.concatenate([back_ref[j, w * 32 : (w + 1) * 32, :] for j in range(8)], axis=0)
            lifted[w * 128 : (w + 1) * 128, :] = tn(r, wd_ref[...])

    skips = []
    for g in range(TB // 4):
        dec = []
        for k in range(4):
            s = 4 * g + k
            lift = lifted[pl.ds(step * TB + s, 8, stride=128), :]
            lift = jnp.where(child_ref[step * TB + s] >= 0, lift, -3e38)
            h = hid_ref[s * 64 : (s + 1) * 64, :].astype(F32).reshape(8, 8, 128)
            dec.append(jnp.maximum(h + lift[None], 0.0).reshape(64, 128).astype(BF))
        skips.append(nt(ws_ref[...], jnp.concatenate(dec, axis=0)).astype(BF))
    skip = jnp.concatenate(skips, axis=0)
    for k in range(4):
        r = mm(skip, up[k])
        for g in range(TB // 4):
            s = 4 * g + k
            out_ref[s] = (x_ref[s].astype(F32) + r[g * 64 : (g + 1) * 64]).astype(BF)


def shards(
    fine_feats, fine_child, parent_block, w_parent, w_root_in, w_root, root_bias, w_down, w_skip
):
    rows = lax.axis_size("row")
    wc = w_root.transpose(2, 3, 4, 0, 1).reshape(864, 256)
    vm = pl.BlockSpec(memory_space=pltpu.VMEM)
    anym = pl.BlockSpec(memory_space=pl.ANY)
    dma = pltpu.SemaphoreType.DMA
    hidden, back, nat = pl.pallas_call(
        functools.partial(root_kernel, rows),
        name="root",
        out_shape=(
            jax.ShapeDtypeStruct((SLOTS * 64, 128), BF),
            jax.ShapeDtypeStruct((8, 256, 128), BF),
            jax.ShapeDtypeStruct((4, 32, 1024), BF),
        ),
        in_specs=[vm, vm, anym, vm, vm, vm, vm],
        out_specs=(anym, anym, vm),
        scratch_shapes=[
            pltpu.VMEM((NB, SB, 64, 512), BF),
            pltpu.VMEM((4, 512, 256), BF),
            pltpu.VMEM((NB * SB * 64, 128), BF),
            pltpu.VMEM((SB * 8, 128), F32),
            pltpu.VMEM((8, 8, 128), I32),
            pltpu.VMEM((1024, 1024), BF),
            pltpu.VMEM((512, 1024), BF),
            pltpu.VMEM((512, 1024), BF),
            pltpu.VMEM((2, 256, 512), BF),
            pltpu.VMEM((6, 4, 256, 256), BF),
            pltpu.VMEM((4, 288, 256), F32),
            pltpu.VMEM((256, 512), BF),
            pltpu.VMEM((128, 1024), BF),
            pltpu.VMEM((1024, 1024), BF),
            pltpu.VMEM((8, 256, 128), BF),
            dma((NB,)),
            dma((NB,)),
            dma((8,)),
            dma((8,)),
            dma((NB, 4)),
            dma((NB, 4)),
            dma((NB, 4)),
            dma((NB, 4)),
            dma((2,)),
            dma((2,)),
            dma((8,)),
            dma((8,)),
            dma,
        ],
        compiler_params=pltpu.CompilerParams(
            collective_id=0, has_side_effects=True, vmem_limit_bytes=60 * 1024 * 1024
        ),
    )(
        fine_child.reshape(1, SLOTS),
        parent_block.reshape(1, 8),
        fine_feats,
        w_parent,
        w_root_in,
        wc,
        root_bias.reshape(1, 32),
    )
    full = lambda shape: pl.BlockSpec(shape, lambda i: (0,) * len(shape))
    fine_out = pl.pallas_call(
        fine_kernel,
        name="fine",
        grid=(SLOTS // TB,),
        out_shape=jax.ShapeDtypeStruct((SLOTS, 64, 512), BF),
        in_specs=[
            pl.BlockSpec(memory_space=pltpu.SMEM),
            pl.BlockSpec((TB, 64, 512), lambda i: (i, 0, 0)),
            pl.BlockSpec((TB * 64, 128), lambda i: (i, 0)),
            full((8, 256, 128)),
            full((256, 128)),
            full((64, 128)),
        ],
        out_specs=pl.BlockSpec((TB, 64, 512), lambda i: (i, 0, 0)),
        scratch_shapes=[pltpu.VMEM((4, 256, 512), BF), pltpu.VMEM((1024, 128), F32)],
        compiler_params=pltpu.CompilerParams(vmem_limit_bytes=48 * 1024 * 1024),
    )(fine_child, fine_feats, hidden, back, w_down, w_skip.T)
    root_local = nat.transpose(1, 0, 2).reshape(32, 4, 32, 32)
    return (fine_out, root_local)


def solution(mesh):
    return jax.shard_map(
        shards,
        mesh=mesh,
        in_specs=(
            P(("row", "ga"), None, None),
            P(("row", "ga")),
            P(("row", "ga")),
            P(),
            P(),
            P("ga", None, None, None, None),
            P("ga"),
            P(),
            P(),
        ),
        out_specs=(P(("row", "ga"), None, None), P("ga", "row", None, None)),
        check_vma=False,
    )
```

```python
import functools

import jax
import jax.numpy as jnp
from jax import lax
from jax.experimental import pallas as pl
from jax.experimental.pallas import tpu as pltpu
from jax.sharding import PartitionSpec as P

BF = jnp.bfloat16
F32 = jnp.float32
I32 = jnp.int32
MESH = pl.DeviceIdType.MESH
SLOTS = 120
NB = 4
SB = 32
TB = 24
OUT = jax.ShapeDtypeStruct
ROOT_MB = 40
FINE_MB = 24


def in_hbm(a):
    return pltpu.with_memory_space_constraint(a, pltpu.HBM)


def iota(shape, dim):
    return lax.broadcasted_iota(I32, shape, dim)


def column_of(v):
    z, y, x = v >> 6, (v >> 3) & 7, v & 7
    w = (z >> 2) * 4 + (y >> 2) * 2 + (x >> 2)
    g = ((z >> 1) & 1) * 4 + ((y >> 1) & 1) * 2 + ((x >> 1) & 1)
    return g * 8 + w


def nt(a, b):
    return lax.dot_general(a, b, (((1,), (1,)), ((), ())), preferred_element_type=F32)


def tn(a, b):
    return lax.dot_general(a, b, (((0,), (0,)), ((), ())), preferred_element_type=F32)


def mm(a, b):
    return jnp.dot(a, b, preferred_element_type=F32)


def root_kernel(
    rows,
    child_hbm,
    block_hbm,
    x_hbm,
    wp_hbm,
    win_hbm,
    wc_hbm,
    bias_hbm,
    x_ref,
    hid_ref,
    back_ref,
    feat_ref,
    child_ref,
    block_ref,
    wp_ref,
    win_ref,
    wc_ref,
    bias_ref,
    p8,
    pp,
    ints,
    gathered,
    place,
    slab,
    halo,
    weff,
    taps,
    rft,
    quad,
    perm,
    flat,
    msgs,
    x_sem,
    w_sem,
    int_send,
    int_recv,
    ag_send,
    ag_recv,
    fw_send,
    fw_recv,
    halo_send,
    halo_recv,
    back_send,
    back_recv,
    own_sem,
):
    row = lax.axis_index("row")
    me = lax.axis_index("ga")
    chip = me // 2
    core = lax.rem(me, 2)
    partner = 2 * chip + 1 - core
    last = rows - 1

    def peer(k):
        return lax.rem(me + k, 8)

    def chip_peer(k):
        return 2 * lax.rem(chip + k, 4) + core

    def remote(src, dst, send, recv, row_at, ga):
        return pltpu.make_async_remote_copy(
            src, dst, send, recv, device_id=(row_at, ga), device_id_type=MESH
        )

    x_copies = []
    for blk in range(NB):
        n = min(SB, SLOTS - blk * SB)
        part = pl.ds(blk * SB, n)
        x_copies.append(pltpu.make_async_copy(x_hbm.at[part], x_ref.at[part], x_sem.at[blk]))
        x_copies[-1].start()

    pairs = [
        (child_hbm, child_ref),
        (block_hbm, block_ref),
        (wp_hbm, wp_ref),
        (win_hbm, win_ref),
        (wc_hbm, wc_ref),
        (bias_hbm, bias_ref),
    ]
    small = [pltpu.make_async_copy(p, q, w_sem.at[i]) for i, (p, q) in enumerate(pairs)]
    for c in small:
        c.start()

    barrier = pltpu.get_barrier_semaphore()
    for k in range(1, 8):
        pl.semaphore_signal(barrier, inc=1, device_id=(row, peer(k)), device_id_type=MESH)

    @pl.when(row > 0)
    def _():
        pl.semaphore_signal(barrier, inc=1, device_id=(row - 1, me), device_id_type=MESH)

    @pl.when(row < last)
    def _():
        pl.semaphore_signal(barrier, inc=1, device_id=(row + 1, me), device_id_type=MESH)

    where = column_of(iota((512, 256), 0))
    lane = iota((512, 256), 1)
    for k in range(4):
        p8[k * 512 : (k + 1) * 512] = jnp.where(lane == where + 64 * k, 0.125, 0.0).astype(BF)
    small[0].wait()
    small[1].wait()
    ints[me] = jnp.full((8, 128), -1, I32)
    ints[me, 0:1, 0:SLOTS] = child_ref[...]
    ints[me, 1:2, 0:8] = block_ref[...]
    small[2].wait()

    int_copies, ag_sent, fw_copies = [], [], []

    def piece(ga, blk):
        return gathered.at[pl.ds(pl.multiple_of(ga * 128 + blk * SB, SB), SB)]

    def forward(ga, blk, k):
        c = remote(
            piece(ga, blk), piece(ga, blk), fw_send.at[blk, k], fw_recv.at[blk, k], row, partner
        )
        c.start()
        fw_copies.append(c)

    def send(ga, blk, k, to):
        c = remote(
            piece(ga, blk), piece(ga, blk), ag_send.at[blk, k], ag_recv.at[blk, k], row, to
        )
        c.start()
        ag_sent.append(c)

    def arrived(ga, blk, k):
        remote(
            piece(me, blk), piece(ga, blk), ag_send.at[blk, k], ag_recv.at[blk, k], row, partner
        ).wait_recv()

    right, left, far = chip_peer(1), chip_peer(3), chip_peer(2)

    def relay(blk):
        first, onward = (0, right) if blk % 2 == 0 else (1, left)
        for k in (first, 1 - first):
            src = left if k == 0 else right
            arrived(src, blk, k)
            if k == first:
                send(src, blk, 2, onward)
            forward(src, blk, 1 + k)

    def far_block(blk):
        arrived(far, blk, 2)
        forward(far, blk, 3)

    for blk in range(NB):
        x_copies[blk].wait()
        n = min(SB, SLOTS - blk * SB)
        x = jnp.concatenate(
            [
                jnp.concatenate([x_ref[blk * SB + 4 * g + k] for k in range(4)], axis=1)
                for g in range(n // 4)
            ],
            axis=0,
        )
        pooled = mm(x, p8[...]).astype(BF)
        for g in range(n // 4):
            h = tn(pooled[g * 64 : (g + 1) * 64], wp_ref[...])
            h = jnp.maximum(h, 0.0).astype(BF)
            hid_ref[pl.ds((blk * SB + 4 * g) * 64, 256), :] = h
            mean = jnp.sum(h.astype(F32).reshape(4, 8, 8, 128), axis=1) * 0.125
            pp[pl.ds(g * 32, 32), :] = mean.reshape(32, 128)
        if n < SB:
            pp[pl.ds(n * 8, (SB - n) * 8), :] = jnp.zeros(((SB - n) * 8, 128), F32)
        start = pl.multiple_of(me * 128 + blk * SB, SB)
        for w in range(8):
            gathered[pl.ds(start, SB), w * 128 : (w + 1) * 128] = pp[
                pl.ds(w, SB, stride=8), :
            ].astype(BF)
        if blk == 0:
            sides = (row > 0).astype(I32) + (row < last).astype(I32)
            pl.semaphore_wait(barrier, 7 + sides)
        send(me, blk, 0, right)
        send(me, blk, 1, left)
        forward(me, blk, 0)
        if blk == 0:
            for k in range(1, 8):
                c = remote(ints.at[me], ints.at[me], int_send.at[k], int_recv.at[k], row, peer(k))
                c.start()
                int_copies.append(c)
        else:
            relay(blk - 1)
        if blk >= 2:
            far_block(blk - 2)

    for c in small[3:]:
        c.wait()
    weff[...] = nt(wc_ref[...], win_ref[...]).astype(BF)

    for c in int_copies:
        c.wait()
    child = jnp.concatenate([ints[m, 0:1, :] for m in range(8)], axis=0)
    parent = child >> 3
    block = jnp.zeros((8, 128), I32)
    for m in range(8):
        blocks = ints[m, 1:2, :]
        for i in range(8):
            block = jnp.where(parent == 8 * m + i, blocks[:, i : i + 1], block)
    octant = child & 7
    pos = (
        (octant >> 2) * 256
        + (2 * (block >> 3) + ((octant >> 1) & 1)) * 16
        + 2 * (block & 7)
        + (octant & 1)
    )
    pos = jnp.where(child >= 0, pos, -1)

    relay(NB - 1)
    far_block(NB - 2)
    for m in range(8):
        hot = iota((512, 128), 0) == pos[m : m + 1, :]
        place[:, m * 128 : (m + 1) * 128] = jnp.where(hot, 1.0, 0.0).astype(BF)
    far_block(NB - 1)
    for c in fw_copies:
        c.wait_recv()

    def put(half, i):
        r = pl.ds(half * 256, 256)
        c = slice(i * 256, (i + 1) * 256)
        slab[r, c] = mm(place[r, :], gathered[:, c]).astype(BF)

    low = remote(
        slab.at[pl.ds(0, 256), pl.ds(0, 512)],
        halo.at[1],
        halo_send.at[0],
        halo_recv.at[1],
        jnp.maximum(row - 1, 0),
        me,
    )
    high = remote(
        slab.at[pl.ds(256, 256), pl.ds(512, 512)],
        halo.at[0],
        halo_send.at[1],
        halo_recv.at[0],
        jnp.minimum(row + 1, last),
        me,
    )
    put(0, 0)
    put(0, 1)

    @pl.when(row > 0)
    def _():
        low.start()

    put(1, 2)
    put(1, 3)

    @pl.when(row < last)
    def _():
        high.start()

    put(0, 2)
    put(0, 3)
    put(1, 0)
    put(1, 1)

    spot = iota((32, 256), 1)
    oy, ox = spot >> 4, spot & 15
    bias = jnp.sum(
        jnp.where(iota((32, 32), 0) == iota((32, 32), 1), bias_ref[...], 0.0),
        axis=1,
        keepdims=True,
    )

    def plane(zz, ab):
        c = ((zz & 1) * 4 + ab) * 128
        return slab[pl.ds((zz >> 1) * 256, 256), c : c + 128]

    def weights(lo, hi):
        return jnp.concatenate([weff[d * 288 : (d + 1) * 288] for d in range(lo, hi)], axis=1)

    def matmuls(z):
        lo, hi = max(0, 1 - z), min(3, 5 - z)
        for ab in range(4):
            x = jnp.concatenate([plane(z - 1 + d, ab) for d in range(lo, hi)], axis=1)
            taps[z, ab] = nt(weights(lo, hi), x)

    def outer(z, side):
        d = 0 if side == 0 else 2
        for ab in range(4):
            x = halo[side, :, ab * 128 : (ab + 1) * 128]
            taps[z, ab] += nt(weights(d, d + 1), x)

    def combine(z):
        def tap(a, b, dy, dx):
            t = ((dy + 1) * 3 + dx + 1) * 32
            return taps[z, 2 * a + b, t : t + 32, :]

        for iy in range(2):
            for ix in range(2):
                ys = [(iy, 0), (1 - iy, 1 - 2 * iy)]
                xs = [(ix, 0), (1 - ix, 1 - 2 * ix)]
                ysh = (1 - iy, 2 * iy - 1)
                xsh = (1 - ix, 2 * ix - 1)
                plain = sum(tap(a, b, dy, dx) for a, dy in ys for b, dx in xs)
                only_x = sum(tap(a, xsh[0], dy, xsh[1]) for a, dy in ys)
                only_y = sum(tap(ysh[0], b, ysh[1], dx) for b, dx in xs)
                both = tap(ysh[0], xsh[0], ysh[1], xsh[1])

                def shift_x(v):
                    v = pltpu.roll(v, 255 if ix else 1, 1)
                    return jnp.where(ox == (15 if ix else 0), 0.0, v)

                def shift_y(v):
                    v = pltpu.roll(v, 240 if iy else 16, 1)
                    return jnp.where(oy == (15 if iy else 0), 0.0, v)

                total = plain + shift_x(only_x) + shift_y(only_y + shift_x(both))
                out = jnp.maximum(total + bias, 0.0).astype(BF)
                w = (z & 1) * 4 + iy * 2 + ix
                rft[w * 32 : (w + 1) * 32, (z >> 1) * 256 : ((z >> 1) + 1) * 256] = out
                r = iy * 128 + z * 32
                quad[r : r + 32, ix * 256 : (ix + 1) * 256] = out

    matmuls(1)
    matmuls(2)
    combine(1)
    combine(2)
    matmuls(0)
    matmuls(3)
    p, q = iota((512, 512), 0), iota((512, 512), 1)
    hot = q == ((p >> 4) & 15) * 32 + 2 * (p & 15) + (p >> 8)
    perm[...] = jnp.where(hot, 1.0, 0.0).astype(BF)

    @pl.when(row > 0)
    def _():
        high.wait_recv()

    @pl.when(row < last)
    def _():
        low.wait_recv()

    @pl.when(row == 0)
    def _():
        halo[0] = jnp.zeros((256, 512), BF)

    @pl.when(row == last)
    def _():
        halo[1] = jnp.zeros((256, 512), BF)

    outer(0, 0)
    outer(3, 1)
    combine(0)
    combine(3)

    for i in range(4):
        m2 = mm(rft[...], place[:, i * 256 : (i + 1) * 256]).astype(BF)
        msgs[2 * i] = m2[:, :128]
        msgs[2 * i + 1] = m2[:, 128:]
    back_copies = []
    for k in (4, 3, 5, 2, 6, 1, 7):
        c = remote(
            msgs.at[peer(k)], back_ref.at[me], back_send.at[k], back_recv.at[k], row, peer(k)
        )
        c.start()
        back_copies.append(c)
    own = pltpu.make_async_copy(msgs.at[me], back_ref.at[me], own_sem)
    own.start()

    nat = mm(quad[...], perm[...])
    for iy in range(2):
        for z in range(4):
            v = nat[iy * 128 + z * 32 : iy * 128 + z * 32 + 32]
            for t in range(16):
                tile = v[:, t // 4 * 128 : t // 4 * 128 + 128]
                if t % 4:
                    tile = pltpu.roll(tile, 128 - 32 * (t % 4), 1)
                flat[pl.ds(z * 32 + 2 * t + iy, 32, stride=128), :] = tile
    for c in range(32):
        f = flat[c * 128 : (c + 1) * 128, :][:, :32].astype(BF)
        feat_ref[c] = f.reshape(4, 32, 32)

    for c in ag_sent:
        c.wait_send()
    for c in fw_copies:
        c.wait_send()

    @pl.when(row > 0)
    def _():
        low.wait_send()

    @pl.when(row < last)
    def _():
        high.wait_send()

    own.wait()
    for c in back_copies:
        c.wait()


def fine_kernel(
    child_ref, x_ref, hid_ref, back_ref, wd_ref, ws_ref, feat_ref, out_ref, root_ref, up, lifted, sem
):
    step = pl.program_id(0)
    copy = pltpu.make_async_copy(feat_ref, root_ref, sem)

    @pl.when(step == 0)
    def _():
        copy.start()
        where = column_of(iota((256, 512), 1))
        line = iota((256, 512), 0)
        for k in range(4):
            up[k] = jnp.where(line == where + 64 * k, 1.0, 0.0).astype(BF)
        for w in range(8):
            r = jnp.concatenate([back_ref[j, w * 32 : (w + 1) * 32, :] for j in range(8)], axis=0)
            lifted[w * 128 : (w + 1) * 128, :] = tn(r, wd_ref[...])

    skips = []
    for g in range(TB // 4):
        dec = []
        for k in range(4):
            s = step * TB + 4 * g + k
            lift = lifted[pl.ds(s, 8, stride=128), :]
            lift = jnp.where(child_ref[s] >= 0, lift, -3e38)
            h = hid_ref[pl.ds(pl.multiple_of(s * 64, 64), 64), :].astype(F32).reshape(8, 8, 128)
            dec.append(jnp.maximum(h + lift[None], 0.0).reshape(64, 128).astype(BF))
        skips.append(nt(ws_ref[...], jnp.concatenate(dec, axis=0)).astype(BF))
    skip = jnp.concatenate(skips, axis=0)
    for k in range(4):
        r = mm(skip, up[k])
        for g in range(TB // 4):
            s = 4 * g + k
            x = x_ref[step * TB + s].astype(F32)
            out_ref[s] = (x + r[g * 64 : (g + 1) * 64]).astype(BF)

    @pl.when(step == SLOTS // TB - 1)
    def _():
        copy.wait()


def shards(
    fine_feats, fine_child, parent_block, w_parent, w_root_in, w_root, root_bias, w_down, w_skip
):
    rows = lax.axis_size("row")
    wc = w_root.transpose(2, 3, 4, 0, 1).reshape(864, 256)
    vm = pl.BlockSpec(memory_space=pltpu.VMEM)
    anym = pl.BlockSpec(memory_space=pl.ANY)
    hbm = pl.BlockSpec(memory_space=pltpu.HBM)
    dma = pltpu.SemaphoreType.DMA
    x, hidden, back, feat = pl.pallas_call(
        functools.partial(root_kernel, rows),
        name="root",
        out_shape=(
            OUT((SLOTS, 64, 512), BF),
            OUT((SLOTS * 64, 128), BF),
            OUT((8, 256, 128), BF),
            OUT((32, 4, 32, 32), BF),
        ),
        in_specs=[hbm] * 7,
        out_specs=(vm, vm, vm, vm),
        scratch_shapes=[
            pltpu.VMEM((1, SLOTS), I32),
            pltpu.VMEM((1, 8), I32),
            pltpu.VMEM((64, 128), BF),
            pltpu.VMEM((128, 256), BF),
            pltpu.VMEM((864, 256), BF),
            pltpu.VMEM((1, 32), F32),
            pltpu.VMEM((2048, 256), BF),
            pltpu.VMEM((SB * 8, 128), F32),
            pltpu.VMEM((8, 8, 128), I32),
            pltpu.VMEM((1024, 1024), BF),
            pltpu.VMEM((512, 1024), BF),
            pltpu.VMEM((512, 1024), BF),
            pltpu.VMEM((2, 256, 512), BF),
            pltpu.VMEM((864, 128), BF),
            pltpu.VMEM((4, 4, 288, 256), F32),
            pltpu.VMEM((256, 512), BF),
            pltpu.VMEM((256, 512), BF),
            pltpu.VMEM((512, 512), BF),
            pltpu.VMEM((4096, 128), F32),
            pltpu.VMEM((8, 256, 128), BF),
            dma((NB,)),
            dma((6,)),
            dma((8,)),
            dma((8,)),
            dma((NB, 3)),
            dma((NB, 3)),
            dma((NB, 4)),
            dma((NB, 4)),
            dma((2,)),
            dma((2,)),
            dma((8,)),
            dma((8,)),
            dma,
        ],
        compiler_params=pltpu.CompilerParams(
            collective_id=0, has_side_effects=True, vmem_limit_bytes=ROOT_MB * 1024 * 1024
        ),
    )(
        in_hbm(fine_child.reshape(1, SLOTS)),
        in_hbm(parent_block.reshape(1, 8)),
        in_hbm(fine_feats),
        in_hbm(w_parent),
        in_hbm(w_root_in),
        in_hbm(wc),
        in_hbm(root_bias.reshape(1, 32)),
    )
    return pl.pallas_call(
        fine_kernel,
        name="fine",
        grid=(SLOTS // TB,),
        out_shape=(
            jax.ShapeDtypeStruct((SLOTS, 64, 512), BF),
            jax.ShapeDtypeStruct((32, 4, 32, 32), BF),
        ),
        in_specs=[pl.BlockSpec(memory_space=pltpu.SMEM), vm, vm, vm, vm, vm, anym],
        out_specs=(pl.BlockSpec((TB, 64, 512), lambda i: (i, 0, 0)), anym),
        scratch_shapes=[
            pltpu.VMEM((4, 256, 512), BF),
            pltpu.VMEM((1024, 128), F32),
            pltpu.SemaphoreType.DMA,
        ],
        compiler_params=pltpu.CompilerParams(vmem_limit_bytes=FINE_MB * 1024 * 1024),
    )(fine_child, x, hidden, back, w_down, w_skip.T, feat)


def solution(mesh):
    return jax.shard_map(
        shards,
        mesh=mesh,
        in_specs=(
            P(("row", "ga"), None, None),
            P(("row", "ga")),
            P(("row", "ga")),
            P(),
            P(),
            P("ga", None, None, None, None),
            P("ga"),
            P(),
            P(),
        ),
        out_specs=(P(("row", "ga"), None, None), P("ga", "row", None, None)),
        check_vma=False,
    )
```

```python
import functools

import jax
import jax.numpy as jnp
from jax import lax
from jax.experimental import pallas as pl
from jax.experimental.pallas import tpu as pltpu
from jax.sharding import PartitionSpec as P

BF = jnp.bfloat16
F32 = jnp.float32
I32 = jnp.int32
MESH = pl.DeviceIdType.MESH
SLOTS = 120
BLOCKS = ((0, 16, 16), (16, 32, 32), (48, 32, 32), (80, 32, 32), (112, 8, 16))
NB = len(BLOCKS)
TB = 24
OUT = jax.ShapeDtypeStruct
ROOT_MB = 40
FINE_MB = 24


def in_hbm(a):
    return pltpu.with_memory_space_constraint(a, pltpu.HBM)


def iota(shape, dim):
    return lax.broadcasted_iota(I32, shape, dim)


def column_of(v):
    z, y, x = v >> 6, (v >> 3) & 7, v & 7
    w = (z >> 2) * 4 + (y >> 2) * 2 + (x >> 2)
    g = ((z >> 1) & 1) * 4 + ((y >> 1) & 1) * 2 + ((x >> 1) & 1)
    return g * 8 + w


def nt(a, b):
    return lax.dot_general(a, b, (((1,), (1,)), ((), ())), preferred_element_type=F32)


def tn(a, b):
    return lax.dot_general(a, b, (((0,), (0,)), ((), ())), preferred_element_type=F32)


def mm(a, b):
    return jnp.dot(a, b, preferred_element_type=F32)


def root_kernel(
    rows,
    child_hbm,
    block_hbm,
    x_hbm,
    wp_hbm,
    win_hbm,
    wc_hbm,
    bias_hbm,
    x_ref,
    hid_ref,
    back_ref,
    feat_ref,
    child_ref,
    block_ref,
    wp_ref,
    win_ref,
    wc_ref,
    bias_ref,
    p8,
    pp,
    ints,
    gathered,
    place,
    slab,
    halo,
    weff,
    taps,
    rft,
    quad,
    perm,
    flat,
    msgs,
    x_sem,
    w_sem,
    int_send,
    int_recv,
    ag_send,
    ag_recv,
    fw_send,
    fw_recv,
    halo_send,
    halo_recv,
    swap_send,
    swap_recv,
    back_send,
    back_recv,
    own_sem,
):
    row = lax.axis_index("row")
    me = lax.axis_index("ga")
    chip = me // 2
    core = lax.rem(me, 2)
    partner = 2 * chip + 1 - core
    last = rows - 1

    def peer(k):
        return lax.rem(me + k, 8)

    def chip_peer(k):
        return 2 * lax.rem(chip + k, 4) + core

    def remote(src, dst, send, recv, row_at, ga):
        return pltpu.make_async_remote_copy(
            src, dst, send, recv, device_id=(row_at, ga), device_id_type=MESH
        )

    x_copies = []
    for blk, (first, n, _) in enumerate(BLOCKS):
        part = pl.ds(first, n)
        x_copies.append(pltpu.make_async_copy(x_hbm.at[part], x_ref.at[part], x_sem.at[blk]))
        x_copies[-1].start()

    pairs = [
        (child_hbm, child_ref),
        (block_hbm, block_ref),
        (wp_hbm, wp_ref),
        (win_hbm, win_ref),
        (wc_hbm, wc_ref),
        (bias_hbm, bias_ref),
    ]
    small = [pltpu.make_async_copy(p, q, w_sem.at[i]) for i, (p, q) in enumerate(pairs)]
    for c in small:
        c.start()

    barrier = pltpu.get_barrier_semaphore()
    for k in range(1, 8):
        pl.semaphore_signal(barrier, inc=1, device_id=(row, peer(k)), device_id_type=MESH)

    @pl.when(row > 0)
    def _():
        pl.semaphore_signal(barrier, inc=1, device_id=(row - 1, me), device_id_type=MESH)

    @pl.when(row < last)
    def _():
        pl.semaphore_signal(barrier, inc=1, device_id=(row + 1, me), device_id_type=MESH)

    where = column_of(iota((512, 256), 0))
    lane = iota((512, 256), 1)
    for k in range(4):
        p8[k * 512 : (k + 1) * 512] = jnp.where(lane == where + 64 * k, 0.125, 0.0).astype(BF)
    small[0].wait()
    small[1].wait()
    ints[me] = jnp.full((8, 128), -1, I32)
    ints[me, 0:1, 0:SLOTS] = child_ref[...]
    ints[me, 1:2, 0:8] = block_ref[...]
    small[2].wait()

    int_copies, ag_sent, fw_copies = [], [], []

    def piece(ga, blk):
        first, _, sent = BLOCKS[blk]
        return gathered.at[pl.ds(pl.multiple_of(ga * 128 + first, 16), sent)]

    def forward(ga, blk, k):
        c = remote(
            piece(ga, blk), piece(ga, blk), fw_send.at[blk, k], fw_recv.at[blk, k], row, partner
        )
        c.start()
        fw_copies.append(c)

    def send(ga, blk, k, to):
        c = remote(
            piece(ga, blk), piece(ga, blk), ag_send.at[blk, k], ag_recv.at[blk, k], row, to
        )
        c.start()
        ag_sent.append(c)

    right, left, far = chip_peer(1), chip_peer(3), chip_peer(2)
    relays = {1: (0, right), 2: (1, left)}
    origin = (left, right, far)

    def arrived(blk, k):
        ga = origin[k]
        remote(
            piece(me, blk), piece(ga, blk), ag_send.at[blk, k], ag_recv.at[blk, k], row, partner
        ).wait_recv()
        if blk in relays and relays[blk][0] == k:
            send(ga, blk, 2, relays[blk][1])
        forward(ga, blk, 1 + k)

    for blk, (first, n, sent) in enumerate(BLOCKS):
        x_copies[blk].wait()
        x = jnp.concatenate(
            [
                jnp.concatenate([x_ref[first + 4 * g + k] for k in range(4)], axis=1)
                for g in range(n // 4)
            ],
            axis=0,
        )
        pooled = mm(x, p8[...]).astype(BF)
        for g in range(n // 4):
            h = tn(pooled[g * 64 : (g + 1) * 64], wp_ref[...])
            h = jnp.maximum(h, 0.0).astype(BF)
            hid_ref[pl.ds((first + 4 * g) * 64, 256), :] = h
            mean = jnp.sum(h.astype(F32).reshape(4, 8, 8, 128), axis=1) * 0.125
            pp[pl.ds(g * 32, 32), :] = mean.reshape(32, 128)
        if n < sent:
            pp[pl.ds(n * 8, (sent - n) * 8), :] = jnp.zeros(((sent - n) * 8, 128), F32)
        start = pl.multiple_of(me * 128 + first, 16)
        for w in range(8):
            gathered[pl.ds(start, sent), w * 128 : (w + 1) * 128] = pp[
                pl.ds(w, sent, stride=8), :
            ].astype(BF)
        if blk == 0:
            sides = (row > 0).astype(I32) + (row < last).astype(I32)
            pl.semaphore_wait(barrier, 7 + sides)
        if blk not in relays:
            send(me, blk, 2, far)
        send(me, blk, 0, right)
        send(me, blk, 1, left)
        forward(me, blk, 0)
        if blk == 0:
            for k in range(1, 8):
                c = remote(ints.at[me], ints.at[me], int_send.at[k], int_recv.at[k], row, peer(k))
                c.start()
                int_copies.append(c)
        if blk >= 3:
            arrived(blk - 2, relays[blk - 2][0])

    for c in small[3:]:
        c.wait()
    weff[...] = nt(wc_ref[...], win_ref[...]).astype(BF)

    for c in int_copies:
        c.wait()
    child = jnp.concatenate([ints[m, 0:1, :] for m in range(8)], axis=0)
    parent = child >> 3
    block = jnp.zeros((8, 128), I32)
    for m in range(8):
        blocks = ints[m, 1:2, :]
        for i in range(8):
            block = jnp.where(parent == 8 * m + i, blocks[:, i : i + 1], block)
    octant = child & 7
    pos = (
        (octant >> 2) * 256
        + (2 * (block >> 3) + ((octant >> 1) & 1)) * 16
        + 2 * (block & 7)
        + (octant & 1)
    )
    pos = jnp.where(child >= 0, pos, -1)

    for m in range(8):
        hot = iota((512, 128), 0) == pos[m : m + 1, :]
        place[:, m * 128 : (m + 1) * 128] = jnp.where(hot, 1.0, 0.0).astype(BF)
    for blk in range(NB):
        for k in (0, 1, 2):
            if blk not in relays or relays[blk][0] != k:
                arrived(blk, k)
    for c in fw_copies:
        c.wait_recv()

    def put(half, i):
        r = pl.ds(half * 256, 256)
        c = slice(i * 256, (i + 1) * 256)
        slab[r, c] = mm(place[r, :], gathered[:, c]).astype(BF)

    near = pl.ds(pl.multiple_of(core * 256, 256), 256)
    low = remote(
        slab.at[pl.ds(0, 256), near],
        halo.at[1, core],
        halo_send.at[0],
        halo_recv.at[1],
        jnp.maximum(row - 1, 0),
        me,
    )
    high = remote(
        slab.at[pl.ds(256, 256), pl.ds(pl.multiple_of(512 + core * 256, 256), 256)],
        halo.at[0, core],
        halo_send.at[1],
        halo_recv.at[0],
        jnp.minimum(row + 1, last),
        me,
    )
    swaps = [
        remote(
            halo.at[side, core],
            halo.at[side, core],
            swap_send.at[side],
            swap_recv.at[side],
            row,
            partner,
        )
        for side in range(2)
    ]
    put(0, 0)
    put(0, 1)

    @pl.when(row > 0)
    def _():
        low.start()

    put(1, 2)
    put(1, 3)

    @pl.when(row < last)
    def _():
        high.start()

    put(0, 2)
    put(0, 3)
    put(1, 0)
    put(1, 1)

    spot = iota((32, 256), 1)
    oy, ox = spot >> 4, spot & 15
    bias = jnp.sum(
        jnp.where(iota((32, 32), 0) == iota((32, 32), 1), bias_ref[...], 0.0),
        axis=1,
        keepdims=True,
    )

    def plane(zz, ab):
        c = ((zz & 1) * 4 + ab) * 128
        return slab[pl.ds((zz >> 1) * 256, 256), c : c + 128]

    def weights(lo, hi):
        return jnp.concatenate([weff[d * 288 : (d + 1) * 288] for d in range(lo, hi)], axis=1)

    def matmuls(z):
        lo, hi = max(0, 1 - z), min(3, 5 - z)
        for ab in range(4):
            x = jnp.concatenate([plane(z - 1 + d, ab) for d in range(lo, hi)], axis=1)
            taps[z, ab] = nt(weights(lo, hi), x)

    def outer(z, side, half):
        d = 0 if side == 0 else 2
        for i in range(2):
            x = halo[side, half, :, i * 128 : (i + 1) * 128]
            taps[z, 2 * half + i] += nt(weights(d, d + 1), x)

    def combine(z):
        def tap(a, b, dy, dx):
            t = ((dy + 1) * 3 + dx + 1) * 32
            return taps[z, 2 * a + b, t : t + 32, :]

        for iy in range(2):
            for ix in range(2):
                ys = [(iy, 0), (1 - iy, 1 - 2 * iy)]
                xs = [(ix, 0), (1 - ix, 1 - 2 * ix)]
                ysh = (1 - iy, 2 * iy - 1)
                xsh = (1 - ix, 2 * ix - 1)
                plain = sum(tap(a, b, dy, dx) for a, dy in ys for b, dx in xs)
                only_x = sum(tap(a, xsh[0], dy, xsh[1]) for a, dy in ys)
                only_y = sum(tap(ysh[0], b, ysh[1], dx) for b, dx in xs)
                both = tap(ysh[0], xsh[0], ysh[1], xsh[1])

                def shift_x(v):
                    v = pltpu.roll(v, 255 if ix else 1, 1)
                    return jnp.where(ox == (15 if ix else 0), 0.0, v)

                def shift_y(v):
                    v = pltpu.roll(v, 240 if iy else 16, 1)
                    return jnp.where(oy == (15 if iy else 0), 0.0, v)

                total = plain + shift_x(only_x) + shift_y(only_y + shift_x(both))
                out = jnp.maximum(total + bias, 0.0).astype(BF)
                r = (iy * 2 + ix) * 32
                part = 0 if z in (1, 2) else 1
                rft[part, r : r + 32, (z >> 1) * 256 : ((z >> 1) + 1) * 256] = out
                r = iy * 128 + z * 32
                quad[r : r + 32, ix * 256 : (ix + 1) * 256] = out

    back_copies, own_copies = [], []

    def give_back(part):
        for i in range(4):
            m2 = mm(rft[part], place[:, i * 256 : (i + 1) * 256]).astype(BF)
            msgs[part, 2 * i] = m2[:, :128]
            msgs[part, 2 * i + 1] = m2[:, 128:]
        for k in (4, 3, 5, 2, 6, 1, 7):
            c = remote(
                msgs.at[part, peer(k)],
                back_ref.at[part, me],
                back_send.at[part, k],
                back_recv.at[part, k],
                row,
                peer(k),
            )
            c.start()
            back_copies.append(c)
        c = pltpu.make_async_copy(msgs.at[part, me], back_ref.at[part, me], own_sem.at[part])
        c.start()
        own_copies.append(c)

    @pl.when(row == 0)
    def _():
        halo[0] = jnp.zeros((2, 256, 256), BF)

    @pl.when(row == last)
    def _():
        halo[1] = jnp.zeros((2, 256, 256), BF)

    matmuls(1)
    matmuls(2)
    combine(1)
    combine(2)
    give_back(0)
    matmuls(0)
    matmuls(3)
    p, q = iota((512, 512), 0), iota((512, 512), 1)
    hot = q == ((p >> 4) & 15) * 32 + 2 * (p & 15) + (p >> 8)
    perm[...] = jnp.where(hot, 1.0, 0.0).astype(BF)

    @pl.when(row > 0)
    def _():
        high.wait_recv()
        swaps[0].start()

    @pl.when(row < last)
    def _():
        low.wait_recv()
        swaps[1].start()

    outer(0, 0, core)
    outer(3, 1, core)

    @pl.when(row > 0)
    def _():
        swaps[0].wait_recv()

    @pl.when(row < last)
    def _():
        swaps[1].wait_recv()

    outer(0, 0, 1 - core)
    outer(3, 1, 1 - core)
    combine(0)
    combine(3)
    give_back(1)

    nat = mm(quad[...], perm[...])
    for iy in range(2):
        for z in range(4):
            v = nat[iy * 128 + z * 32 : iy * 128 + z * 32 + 32]
            for t in range(16):
                tile = v[:, t // 4 * 128 : t // 4 * 128 + 128]
                if t % 4:
                    tile = pltpu.roll(tile, 128 - 32 * (t % 4), 1)
                flat[pl.ds(z * 32 + 2 * t + iy, 32, stride=128), :] = tile
    for c in range(32):
        f = flat[c * 128 : (c + 1) * 128, :][:, :32].astype(BF)
        feat_ref[c] = f.reshape(4, 32, 32)

    for c in ag_sent:
        c.wait_send()
    for c in fw_copies:
        c.wait_send()

    @pl.when(row > 0)
    def _():
        low.wait_send()
        swaps[0].wait_send()

    @pl.when(row < last)
    def _():
        high.wait_send()
        swaps[1].wait_send()

    for c in own_copies:
        c.wait()
    for c in back_copies:
        c.wait()


def fine_kernel(
    child_ref, x_ref, hid_ref, back_ref, wd_ref, ws_ref, feat_ref, out_ref, root_ref, up, lifted, sem
):
    step = pl.program_id(0)
    copy = pltpu.make_async_copy(feat_ref, root_ref, sem)

    @pl.when(step == 0)
    def _():
        copy.start()
        where = column_of(iota((256, 512), 1))
        line = iota((256, 512), 0)
        for k in range(4):
            up[k] = jnp.where(line == where + 64 * k, 1.0, 0.0).astype(BF)
        for i in range(8):
            rows = slice(i % 4 * 32, i % 4 * 32 + 32)
            r = jnp.concatenate([back_ref[i // 4, j, rows, :] for j in range(8)], axis=0)
            lifted[i * 128 : (i + 1) * 128, :] = tn(r, wd_ref[...])

    skips = []
    for g in range(TB // 4):
        dec = []
        for k in range(4):
            s = step * TB + 4 * g + k
            child = child_ref[s]
            lift = lifted[pl.ds(s, 8, stride=128), :]
            lift = jnp.where((child >> 2) & 1 == 0, pltpu.roll(lift, 4, 0), lift)
            lift = jnp.where(child >= 0, lift, -3e38)
            h = hid_ref[pl.ds(pl.multiple_of(s * 64, 64), 64), :].astype(F32).reshape(8, 8, 128)
            dec.append(jnp.maximum(h + lift[None], 0.0).reshape(64, 128).astype(BF))
        skips.append(nt(ws_ref[...], jnp.concatenate(dec, axis=0)).astype(BF))
    skip = jnp.concatenate(skips, axis=0)
    for k in range(4):
        r = mm(skip, up[k])
        for g in range(TB // 4):
            s = 4 * g + k
            x = x_ref[step * TB + s].astype(F32)
            out_ref[s] = (x + r[g * 64 : (g + 1) * 64]).astype(BF)

    @pl.when(step == SLOTS // TB - 1)
    def _():
        copy.wait()


def shards(
    fine_feats, fine_child, parent_block, w_parent, w_root_in, w_root, root_bias, w_down, w_skip
):
    rows = lax.axis_size("row")
    wc = w_root.transpose(2, 3, 4, 0, 1).reshape(864, 256)
    vm = pl.BlockSpec(memory_space=pltpu.VMEM)
    anym = pl.BlockSpec(memory_space=pl.ANY)
    hbm = pl.BlockSpec(memory_space=pltpu.HBM)
    dma = pltpu.SemaphoreType.DMA
    x, hidden, back, feat = pl.pallas_call(
        functools.partial(root_kernel, rows),
        name="root",
        out_shape=(
            OUT((SLOTS, 64, 512), BF),
            OUT((SLOTS * 64, 128), BF),
            OUT((2, 8, 128, 128), BF),
            OUT((32, 4, 32, 32), BF),
        ),
        in_specs=[hbm] * 7,
        out_specs=(vm, vm, vm, vm),
        scratch_shapes=[
            pltpu.VMEM((1, SLOTS), I32),
            pltpu.VMEM((1, 8), I32),
            pltpu.VMEM((64, 128), BF),
            pltpu.VMEM((128, 256), BF),
            pltpu.VMEM((864, 256), BF),
            pltpu.VMEM((1, 32), F32),
            pltpu.VMEM((2048, 256), BF),
            pltpu.VMEM((256, 128), F32),
            pltpu.VMEM((8, 8, 128), I32),
            pltpu.VMEM((1024, 1024), BF),
            pltpu.VMEM((512, 1024), BF),
            pltpu.VMEM((512, 1024), BF),
            pltpu.VMEM((2, 2, 256, 256), BF),
            pltpu.VMEM((864, 128), BF),
            pltpu.VMEM((4, 4, 288, 256), F32),
            pltpu.VMEM((2, 128, 512), BF),
            pltpu.VMEM((256, 512), BF),
            pltpu.VMEM((512, 512), BF),
            pltpu.VMEM((4096, 128), F32),
            pltpu.VMEM((2, 8, 128, 128), BF),
            dma((NB,)),
            dma((6,)),
            dma((8,)),
            dma((8,)),
            dma((NB, 3)),
            dma((NB, 3)),
            dma((NB, 4)),
            dma((NB, 4)),
            dma((2,)),
            dma((2,)),
            dma((2,)),
            dma((2,)),
            dma((2, 8)),
            dma((2, 8)),
            dma((2,)),
        ],
        compiler_params=pltpu.CompilerParams(
            collective_id=0, has_side_effects=True, vmem_limit_bytes=ROOT_MB * 1024 * 1024
        ),
    )(
        in_hbm(fine_child.reshape(1, SLOTS)),
        in_hbm(parent_block.reshape(1, 8)),
        in_hbm(fine_feats),
        in_hbm(w_parent),
        in_hbm(w_root_in),
        in_hbm(wc),
        in_hbm(root_bias.reshape(1, 32)),
    )
    return pl.pallas_call(
        fine_kernel,
        name="fine",
        grid=(SLOTS // TB,),
        out_shape=(
            jax.ShapeDtypeStruct((SLOTS, 64, 512), BF),
            jax.ShapeDtypeStruct((32, 4, 32, 32), BF),
        ),
        in_specs=[pl.BlockSpec(memory_space=pltpu.SMEM), vm, vm, vm, vm, vm, anym],
        out_specs=(pl.BlockSpec((TB, 64, 512), lambda i: (i, 0, 0)), anym),
        scratch_shapes=[
            pltpu.VMEM((4, 256, 512), BF),
            pltpu.VMEM((1024, 128), F32),
            pltpu.SemaphoreType.DMA,
        ],
        compiler_params=pltpu.CompilerParams(vmem_limit_bytes=FINE_MB * 1024 * 1024),
    )(fine_child, x, hidden, back, w_down, w_skip.T, feat)


def solution(mesh):
    return jax.shard_map(
        shards,
        mesh=mesh,
        in_specs=(
            P(("row", "ga"), None, None),
            P(("row", "ga")),
            P(("row", "ga")),
            P(),
            P(),
            P("ga", None, None, None, None),
            P("ga"),
            P(),
            P(),
        ),
        out_specs=(P(("row", "ga"), None, None), P("ga", "row", None, None)),
        check_vma=False,
    )
```

```python
import functools

import jax
import jax.numpy as jnp
from jax import lax
from jax.experimental import pallas as pl
from jax.experimental.pallas import tpu as pltpu
from jax.sharding import PartitionSpec as P

BF = jnp.bfloat16
F32 = jnp.float32
I32 = jnp.int32
MESH = pl.DeviceIdType.MESH
SLOTS = 120
BLOCKS = ((0, 16, 16), (16, 32, 32), (48, 32, 32), (80, 32, 32), (112, 8, 16))
NB = len(BLOCKS)
TB = 24
OUT = jax.ShapeDtypeStruct
ROOT_MB = 40
FINE_MB = 24


def in_hbm(a):
    return pltpu.with_memory_space_constraint(a, pltpu.HBM)


def iota(shape, dim):
    return lax.broadcasted_iota(I32, shape, dim)


def column_of(v):
    z, y, x = v >> 6, (v >> 3) & 7, v & 7
    w = (z >> 2) * 4 + (y >> 2) * 2 + (x >> 2)
    g = ((z >> 1) & 1) * 4 + ((y >> 1) & 1) * 2 + ((x >> 1) & 1)
    return g * 8 + w


def nt(a, b):
    return lax.dot_general(a, b, (((1,), (1,)), ((), ())), preferred_element_type=F32)


def tn(a, b):
    return lax.dot_general(a, b, (((0,), (0,)), ((), ())), preferred_element_type=F32)


def mm(a, b):
    return jnp.dot(a, b, preferred_element_type=F32)


def root_kernel(
    rows,
    child_hbm,
    block_hbm,
    x_hbm,
    wp_hbm,
    win_hbm,
    wc_hbm,
    bias_hbm,
    x_ref,
    hid_ref,
    back_ref,
    feat_ref,
    child_ref,
    block_ref,
    wp_ref,
    win_ref,
    wc_ref,
    bias_ref,
    p8,
    wp4,
    pp,
    ints,
    gathered,
    place,
    slab,
    halo,
    halo_out,
    own,
    weff,
    taps,
    rft,
    quad,
    perm,
    flat,
    msgs,
    x_sem,
    w_sem,
    int_send,
    int_recv,
    ag_send,
    ag_recv,
    fw_send,
    fw_recv,
    halo_send,
    halo_recv,
    back_send,
    back_recv,
    own_sem,
):
    row = lax.axis_index("row")
    me = lax.axis_index("ga")
    chip = me // 2
    core = lax.rem(me, 2)
    partner = 2 * chip + 1 - core
    last = rows - 1

    def peer(k):
        return lax.rem(me + k, 8)

    def chip_peer(k):
        return 2 * lax.rem(chip + k, 4) + core

    def remote(src, dst, send, recv, row_at, ga):
        return pltpu.make_async_remote_copy(
            src, dst, send, recv, device_id=(row_at, ga), device_id_type=MESH
        )

    x_copies = []
    for blk, (first, n, _) in enumerate(BLOCKS):
        part = pl.ds(first, n)
        x_copies.append(pltpu.make_async_copy(x_hbm.at[part], x_ref.at[part], x_sem.at[blk]))
        x_copies[-1].start()

    pairs = [
        (child_hbm, child_ref),
        (block_hbm, block_ref),
        (wp_hbm, wp_ref),
        (win_hbm, win_ref),
        (wc_hbm, wc_ref),
        (bias_hbm, bias_ref),
    ]
    small = [pltpu.make_async_copy(p, q, w_sem.at[i]) for i, (p, q) in enumerate(pairs)]
    for c in small:
        c.start()

    barrier = pltpu.get_barrier_semaphore()
    for k in range(1, 8):
        pl.semaphore_signal(barrier, inc=1, device_id=(row, peer(k)), device_id_type=MESH)

    @pl.when(row > 0)
    def _():
        pl.semaphore_signal(barrier, inc=1, device_id=(row - 1, me), device_id_type=MESH)

    @pl.when(row < last)
    def _():
        pl.semaphore_signal(barrier, inc=1, device_id=(row + 1, me), device_id_type=MESH)

    hot = column_of(iota((1, 512), 1)) == iota((64, 512), 0)
    p8[...] = jnp.where(hot, 0.125, 0.0).astype(BF)
    wp4[...] = jnp.zeros((256, 512), BF)
    small[0].wait()
    small[1].wait()
    ints[me] = jnp.full((8, 128), -1, I32)
    ints[me, 0:1, 0:SLOTS] = child_ref[...]
    ints[me, 1:2, 0:8] = block_ref[...]
    small[2].wait()
    for k in range(4):
        wp4[k * 64 : (k + 1) * 64, k * 128 : (k + 1) * 128] = wp_ref[...]

    int_copies, ag_sent, fw_copies = [], [], []

    def piece(ga, blk):
        first, _, sent = BLOCKS[blk]
        return gathered.at[pl.ds(pl.multiple_of(ga * 128 + first, 16), sent)]

    def forward(ga, blk, k):
        c = remote(
            piece(ga, blk), piece(ga, blk), fw_send.at[blk, k], fw_recv.at[blk, k], row, partner
        )
        c.start()
        fw_copies.append(c)

    def send(ga, blk, k, to):
        c = remote(
            piece(ga, blk), piece(ga, blk), ag_send.at[blk, k], ag_recv.at[blk, k], row, to
        )
        c.start()
        ag_sent.append(c)

    right, left, far = chip_peer(1), chip_peer(3), chip_peer(2)
    relays = {0: (0, right), 1: (1, left), 2: (0, right), 3: (1, left)}
    origin = (left, right, far)

    def arrived(blk, k):
        ga = origin[k]
        remote(
            piece(me, blk), piece(ga, blk), ag_send.at[blk, k], ag_recv.at[blk, k], row, partner
        ).wait_recv()
        if blk in relays and relays[blk][0] == k:
            send(ga, blk, 2, relays[blk][1])
        forward(ga, blk, 1 + k)

    for blk, (first, n, sent) in enumerate(BLOCKS):
        x_copies[blk].wait()
        x = x_ref[first : first + n].reshape(n * 64, 512)
        pooled = nt(p8[...], x).astype(BF)
        pooled = jnp.concatenate(
            [pooled[:, g * 256 : (g + 1) * 256] for g in range(n // 4)], axis=0
        )
        h4 = jnp.maximum(mm(pooled, wp4[...]), 0.0).astype(BF)
        for t in range(n):
            h = h4[t // 4 * 64 : t // 4 * 64 + 64, t % 4 * 128 : t % 4 * 128 + 128]
            hid_ref[pl.ds((first + t) * 64, 64), :] = h
            pp[pl.ds(t * 8, 8), :] = jnp.sum(h.astype(F32).reshape(8, 8, 128), axis=0) * 0.125
        if n < sent:
            pp[pl.ds(n * 8, (sent - n) * 8), :] = jnp.zeros(((sent - n) * 8, 128), F32)
        start = pl.multiple_of(me * 128 + first, 16)
        for w in range(8):
            gathered[pl.ds(start, sent), w * 128 : (w + 1) * 128] = pp[
                pl.ds(w, sent, stride=8), :
            ].astype(BF)
        if blk == 0:
            sides = (row > 0).astype(I32) + (row < last).astype(I32)
            pl.semaphore_wait(barrier, 7 + sides)
        if blk not in relays:
            send(me, blk, 2, far)
        send(me, blk, 0, right)
        send(me, blk, 1, left)
        forward(me, blk, 0)
        if blk == 0:
            for k in range(1, 8):
                c = remote(ints.at[me], ints.at[me], int_send.at[k], int_recv.at[k], row, peer(k))
                c.start()
                int_copies.append(c)
        if blk == 4:
            arrived(0, relays[0][0])

    for c in small[3:]:
        c.wait()
    weff[...] = nt(wc_ref[...], win_ref[...]).astype(BF)

    for c in int_copies:
        c.wait()
    child = jnp.concatenate([ints[m, 0:1, :] for m in range(8)], axis=0)
    parent = child >> 3
    block = jnp.zeros((8, 128), I32)
    for m in range(8):
        blocks = ints[m, 1:2, :]
        for i in range(8):
            block = jnp.where(parent == 8 * m + i, blocks[:, i : i + 1], block)
    octant = child & 7
    pos = (
        (octant >> 2) * 256
        + (2 * (block >> 3) + ((octant >> 1) & 1)) * 16
        + 2 * (block & 7)
        + (octant & 1)
    )
    pos = jnp.where(child >= 0, pos, -1)

    for m in range(8):
        hot = iota((512, 128), 0) == pos[m : m + 1, :]
        place[:, m * 128 : (m + 1) * 128] = jnp.where(hot, 1.0, 0.0).astype(BF)
    order = [(b, k) for b in range(NB) for k in (0, 1)]
    order += [(b, 2) for b in (0, 1, 4, 2, 3)]
    for blk, k in order:
        if (blk, k) != (0, relays[0][0]):
            arrived(blk, k)
    for c in fw_copies:
        c.wait_recv()

    def put(half, i):
        r = pl.ds(half * 256, 256)
        c = slice(i * 512, (i + 1) * 512)
        slab[r, c] = mm(place[r, :], gathered[:, c]).astype(BF)

    low = remote(
        halo_out.at[0],
        halo.at[1],
        halo_send.at[0],
        halo_recv.at[1],
        jnp.maximum(row - 1, 0),
        me,
    )
    high = remote(
        halo_out.at[1],
        halo.at[0],
        halo_send.at[1],
        halo_recv.at[0],
        jnp.minimum(row + 1, last),
        me,
    )

    spot = iota((32, 256), 1)
    oy, ox = spot >> 4, spot & 15
    bias = jnp.sum(
        jnp.where(iota((32, 32), 0) == iota((32, 32), 1), bias_ref[...], 0.0),
        axis=1,
        keepdims=True,
    )

    def plane(zz, ab):
        c = ((zz & 1) * 4 + ab) * 128
        return slab[pl.ds((zz >> 1) * 256, 256), c : c + 128]

    def weights(lo, hi):
        return jnp.concatenate([weff[d * 288 : (d + 1) * 288] for d in range(lo, hi)], axis=1)

    def matmuls(z):
        if z == 4:
            ds, zs = (2, 3), [0]
        elif z == 5:
            ds, zs = (0, 1), [3]
        else:
            ds = (max(0, 1 - z), min(3, 5 - z))
            zs = [z - 1 + d for d in range(*ds)]
        for a in range(2):
            x = [
                jnp.concatenate([plane(zz, 2 * a + b) for zz in zs], axis=1) for b in range(2)
            ]
            r = nt(weights(*ds), jnp.concatenate(x, axis=0))
            taps[z, 2 * a] = r[:, :256]
            taps[z, 2 * a + 1] = r[:, 256:]

    def combine(z):
        def tap(a, b, dy, dx):
            t = ((dy + 1) * 3 + dx + 1) * 32
            return taps[z, 2 * a + b, t : t + 32, :]

        for iy in range(2):
            for ix in range(2):
                ys = [(iy, 0), (1 - iy, 1 - 2 * iy)]
                xs = [(ix, 0), (1 - ix, 1 - 2 * ix)]
                ysh = (1 - iy, 2 * iy - 1)
                xsh = (1 - ix, 2 * ix - 1)
                plain = sum(tap(a, b, dy, dx) for a, dy in ys for b, dx in xs)
                only_x = sum(tap(a, xsh[0], dy, xsh[1]) for a, dy in ys)
                only_y = sum(tap(ysh[0], b, ysh[1], dx) for b, dx in xs)
                both = tap(ysh[0], xsh[0], ysh[1], xsh[1])

                def shift_x(v):
                    v = pltpu.roll(v, 255 if ix else 1, 1)
                    return jnp.where(ox == (15 if ix else 0), 0.0, v)

                def shift_y(v):
                    v = pltpu.roll(v, 240 if iy else 16, 1)
                    return jnp.where(oy == (15 if iy else 0), 0.0, v)

                total = plain + shift_x(only_x) + shift_y(only_y + shift_x(both))
                if z >= 4:
                    halo_out[z - 4, iy * 2 + ix] = total.astype(BF)
                elif z in (0, 3):
                    own[z // 3, iy * 2 + ix] = total + bias
                else:
                    finish(z, iy, ix, total + bias)

    def finish(z, iy, ix, total):
        out = jnp.maximum(total, 0.0).astype(BF)
        r = (iy * 2 + ix) * 32
        part = 0 if z in (1, 2) else 1
        rft[part, r : r + 32, (z >> 1) * 256 : ((z >> 1) + 1) * 256] = out
        r = iy * 128 + z * 32
        quad[r : r + 32, ix * 256 : (ix + 1) * 256] = out

    back_copies, own_copies = [], []

    def give_back(part):
        for i in range(2):
            m4 = mm(rft[part], place[:, i * 512 : (i + 1) * 512]).astype(BF)
            for t in range(4):
                msgs[part, 4 * i + t] = m4[:, t * 128 : (t + 1) * 128]
        for k in (4, 3, 5, 2, 6, 1, 7):
            c = remote(
                msgs.at[part, peer(k)],
                back_ref.at[part, me],
                back_send.at[part, k],
                back_recv.at[part, k],
                row,
                peer(k),
            )
            c.start()
            back_copies.append(c)
        c = pltpu.make_async_copy(msgs.at[part, me], back_ref.at[part, me], own_sem.at[part])
        c.start()
        own_copies.append(c)

    @pl.when(row == 0)
    def _():
        halo[0] = jnp.zeros((4, 32, 256), BF)

    @pl.when(row == last)
    def _():
        halo[1] = jnp.zeros((4, 32, 256), BF)

    put(0, 0)
    matmuls(4)
    combine(4)

    @pl.when(row > 0)
    def _():
        low.start()

    put(1, 1)
    matmuls(5)
    combine(5)

    @pl.when(row < last)
    def _():
        high.start()

    put(0, 1)
    put(1, 0)
    matmuls(1)
    matmuls(2)
    combine(1)
    combine(2)
    give_back(0)
    matmuls(0)
    matmuls(3)
    combine(0)
    combine(3)
    p, q = iota((512, 1), 0), iota((512, 512), 1)
    spread = ((p >> 4) & 15) * 32 + 2 * (p & 15) + (p >> 8)
    perm[...] = jnp.where(q == spread, 1.0, 0.0).astype(BF)

    @pl.when(row > 0)
    def _():
        high.wait_recv()

    @pl.when(row < last)
    def _():
        low.wait_recv()

    for z in (0, 3):
        for iy in range(2):
            for ix in range(2):
                c = iy * 2 + ix
                finish(z, iy, ix, own[z // 3, c] + halo[z // 3, c].astype(F32))
    give_back(1)

    nat = mm(quad[...], perm[...])
    for iy in range(2):
        for z in range(4):
            v = nat[iy * 128 + z * 32 : iy * 128 + z * 32 + 32]
            for t in range(16):
                tile = v[:, t // 4 * 128 : t // 4 * 128 + 128]
                if t % 4:
                    tile = pltpu.roll(tile, 128 - 32 * (t % 4), 1)
                flat[pl.ds(z * 32 + 2 * t + iy, 32, stride=128), :] = tile
    for c in range(32):
        f = flat[c * 128 : (c + 1) * 128, :][:, :32].astype(BF)
        feat_ref[c] = f.reshape(4, 32, 32)

    for c in ag_sent:
        c.wait_send()
    for c in fw_copies:
        c.wait_send()

    @pl.when(row > 0)
    def _():
        low.wait_send()

    @pl.when(row < last)
    def _():
        high.wait_send()

    for c in own_copies:
        c.wait()
    for c in back_copies:
        c.wait()


def fine_kernel(
    child_ref, x_ref, hid_ref, back_ref, wd_ref, ws_ref, feat_ref, out_ref, root_ref, up, lifted, sem
):
    step = pl.program_id(0)
    copy = pltpu.make_async_copy(feat_ref, root_ref, sem)

    @pl.when(step == 0)
    def _():
        copy.start()
        where = column_of(iota((1, 512), 1))
        line = iota((256, 512), 0)
        for k in range(4):
            up[k] = jnp.where(line == where + 64 * k, 1.0, 0.0).astype(BF)
        for i in range(8):
            rows = slice(i % 4 * 32, i % 4 * 32 + 32)
            r = jnp.concatenate([back_ref[i // 4, j, rows, :] for j in range(8)], axis=0)
            lifted[i * 128 : (i + 1) * 128, :] = tn(r, wd_ref[...])

    skips = []
    for g in range(TB // 4):
        dec = []
        for k in range(4):
            s = step * TB + 4 * g + k
            child = child_ref[s]
            lift = lifted[pl.ds(s, 8, stride=128), :]
            lift = jnp.where((child >> 2) & 1 == 0, pltpu.roll(lift, 4, 0), lift)
            lift = jnp.where(child >= 0, lift, -3e38)
            h = hid_ref[pl.ds(pl.multiple_of(s * 64, 64), 64), :].astype(F32).reshape(8, 8, 128)
            dec.append(jnp.maximum(h + lift[None], 0.0).reshape(64, 128).astype(BF))
        skips.append(nt(ws_ref[...], jnp.concatenate(dec, axis=0)).astype(BF))
    skip = jnp.concatenate(skips, axis=0)
    for k in range(4):
        r = mm(skip, up[k])
        for g in range(TB // 4):
            s = 4 * g + k
            x = x_ref[step * TB + s].astype(F32)
            out_ref[s] = (x + r[g * 64 : (g + 1) * 64]).astype(BF)

    @pl.when(step == SLOTS // TB - 1)
    def _():
        copy.wait()


def shards(
    fine_feats, fine_child, parent_block, w_parent, w_root_in, w_root, root_bias, w_down, w_skip
):
    rows = lax.axis_size("row")
    wc = w_root.transpose(2, 3, 4, 0, 1).reshape(864, 256)
    vm = pl.BlockSpec(memory_space=pltpu.VMEM)
    anym = pl.BlockSpec(memory_space=pl.ANY)
    hbm = pl.BlockSpec(memory_space=pltpu.HBM)
    dma = pltpu.SemaphoreType.DMA
    x, hidden, back, feat = pl.pallas_call(
        functools.partial(root_kernel, rows),
        name="root",
        out_shape=(
            OUT((SLOTS, 64, 512), BF),
            OUT((SLOTS * 64, 128), BF),
            OUT((2, 8, 128, 128), BF),
            OUT((32, 4, 32, 32), BF),
        ),
        in_specs=[hbm] * 7,
        out_specs=(vm, vm, vm, vm),
        scratch_shapes=[
            pltpu.VMEM((1, SLOTS), I32),
            pltpu.VMEM((1, 8), I32),
            pltpu.VMEM((64, 128), BF),
            pltpu.VMEM((128, 256), BF),
            pltpu.VMEM((864, 256), BF),
            pltpu.VMEM((1, 32), F32),
            pltpu.VMEM((64, 512), BF),
            pltpu.VMEM((256, 512), BF),
            pltpu.VMEM((256, 128), F32),
            pltpu.VMEM((8, 8, 128), I32),
            pltpu.VMEM((1024, 1024), BF),
            pltpu.VMEM((512, 1024), BF),
            pltpu.VMEM((512, 1024), BF),
            pltpu.VMEM((2, 4, 32, 256), BF),
            pltpu.VMEM((2, 4, 32, 256), BF),
            pltpu.VMEM((2, 4, 32, 256), F32),
            pltpu.VMEM((864, 128), BF),
            pltpu.VMEM((6, 4, 288, 256), F32),
            pltpu.VMEM((2, 128, 512), BF),
            pltpu.VMEM((256, 512), BF),
            pltpu.VMEM((512, 512), BF),
            pltpu.VMEM((4096, 128), F32),
            pltpu.VMEM((2, 8, 128, 128), BF),
            dma((NB,)),
            dma((6,)),
            dma((8,)),
            dma((8,)),
            dma((NB, 3)),
            dma((NB, 3)),
            dma((NB, 4)),
            dma((NB, 4)),
            dma((2,)),
            dma((2,)),
            dma((2, 8)),
            dma((2, 8)),
            dma((2,)),
        ],
        compiler_params=pltpu.CompilerParams(
            collective_id=0, has_side_effects=True, vmem_limit_bytes=ROOT_MB * 1024 * 1024
        ),
    )(
        in_hbm(fine_child.reshape(1, SLOTS)),
        in_hbm(parent_block.reshape(1, 8)),
        in_hbm(fine_feats),
        in_hbm(w_parent),
        in_hbm(w_root_in),
        in_hbm(wc),
        in_hbm(root_bias.reshape(1, 32)),
    )
    return pl.pallas_call(
        fine_kernel,
        name="fine",
        grid=(SLOTS // TB,),
        out_shape=(
            jax.ShapeDtypeStruct((SLOTS, 64, 512), BF),
            jax.ShapeDtypeStruct((32, 4, 32, 32), BF),
        ),
        in_specs=[pl.BlockSpec(memory_space=pltpu.SMEM), vm, vm, vm, vm, vm, anym],
        out_specs=(pl.BlockSpec((TB, 64, 512), lambda i: (i, 0, 0)), anym),
        scratch_shapes=[
            pltpu.VMEM((4, 256, 512), BF),
            pltpu.VMEM((1024, 128), F32),
            pltpu.SemaphoreType.DMA,
        ],
        compiler_params=pltpu.CompilerParams(vmem_limit_bytes=FINE_MB * 1024 * 1024),
    )(fine_child, x, hidden, back, w_down, w_skip.T, feat)


def solution(mesh):
    return jax.shard_map(
        shards,
        mesh=mesh,
        in_specs=(
            P(("row", "ga"), None, None),
            P(("row", "ga")),
            P(("row", "ga")),
            P(),
            P(),
            P("ga", None, None, None, None),
            P("ga"),
            P(),
            P(),
        ),
        out_specs=(P(("row", "ga"), None, None), P("ga", "row", None, None)),
        check_vma=False,
    )
```

```python
import functools

import jax
import jax.numpy as jnp
from jax import lax
from jax.experimental import pallas as pl
from jax.experimental.pallas import tpu as pltpu
from jax.sharding import PartitionSpec as P

BF = jnp.bfloat16
F32 = jnp.float32
I32 = jnp.int32
MESH = pl.DeviceIdType.MESH
SLOTS = 120
BLOCKS = ((0, 16, 16), (16, 32, 32), (48, 32, 32), (80, 32, 32), (112, 8, 16))
NB = len(BLOCKS)
PARTS = ((0, 32), (32, 32), (64, 24), (88, 16), (104, 16))
OUT = jax.ShapeDtypeStruct
ROOT_MB = 40
FINE_MB = 24


def in_hbm(a):
    return pltpu.with_memory_space_constraint(a, pltpu.HBM)


def iota(shape, dim):
    return lax.broadcasted_iota(I32, shape, dim)


def column_of(v):
    z, y, x = v >> 6, (v >> 3) & 7, v & 7
    w = (z >> 2) * 4 + (y >> 2) * 2 + (x >> 2)
    g = ((z >> 1) & 1) * 4 + ((y >> 1) & 1) * 2 + ((x >> 1) & 1)
    return g * 8 + w


def nt(a, b):
    return lax.dot_general(a, b, (((1,), (1,)), ((), ())), preferred_element_type=F32)


def tn(a, b):
    return lax.dot_general(a, b, (((0,), (0,)), ((), ())), preferred_element_type=F32)


def mm(a, b):
    return jnp.dot(a, b, preferred_element_type=F32)


def root_kernel(
    rows,
    child_hbm,
    block_hbm,
    x_hbm,
    wp_hbm,
    win_hbm,
    wc_hbm,
    bias_hbm,
    x_ref,
    hid_ref,
    back_ref,
    feat_ref,
    child_ref,
    block_ref,
    wp_ref,
    win_ref,
    wc_ref,
    bias_ref,
    p8,
    wp4,
    pp,
    ints,
    gathered,
    place,
    slab,
    halo,
    halo_out,
    own,
    weff,
    taps,
    rft,
    quad,
    perm,
    flat,
    msgs,
    x_sem,
    w_sem,
    int_send,
    int_recv,
    ag_send,
    ag_recv,
    fw_send,
    fw_recv,
    halo_send,
    halo_recv,
    back_send,
    back_recv,
    own_sem,
):
    row = lax.axis_index("row")
    me = lax.axis_index("ga")
    chip = me // 2
    core = lax.rem(me, 2)
    partner = 2 * chip + 1 - core
    last = rows - 1

    def peer(k):
        return lax.rem(me + k, 8)

    def chip_peer(k):
        return 2 * lax.rem(chip + k, 4) + core

    def remote(src, dst, send, recv, row_at, ga):
        return pltpu.make_async_remote_copy(
            src, dst, send, recv, device_id=(row_at, ga), device_id_type=MESH
        )

    x_copies = []
    for blk, (first, n, _) in enumerate(BLOCKS):
        part = pl.ds(first, n)
        x_copies.append(pltpu.make_async_copy(x_hbm.at[part], x_ref.at[part], x_sem.at[blk]))
        x_copies[-1].start()

    pairs = [
        (child_hbm, child_ref),
        (block_hbm, block_ref),
        (wp_hbm, wp_ref),
        (win_hbm, win_ref),
        (wc_hbm, wc_ref),
        (bias_hbm, bias_ref),
    ]
    small = [pltpu.make_async_copy(p, q, w_sem.at[i]) for i, (p, q) in enumerate(pairs)]
    for c in small:
        c.start()

    barrier = pltpu.get_barrier_semaphore()
    for k in range(1, 8):
        pl.semaphore_signal(barrier, inc=1, device_id=(row, peer(k)), device_id_type=MESH)

    @pl.when(row > 0)
    def _():
        pl.semaphore_signal(barrier, inc=1, device_id=(row - 1, me), device_id_type=MESH)

    @pl.when(row < last)
    def _():
        pl.semaphore_signal(barrier, inc=1, device_id=(row + 1, me), device_id_type=MESH)

    hot = column_of(iota((1, 512), 1)) == iota((64, 512), 0)
    p8[...] = jnp.where(hot, 0.125, 0.0).astype(BF)
    wp4[...] = jnp.zeros((256, 512), BF)
    small[0].wait()
    small[1].wait()
    ints[me] = jnp.full((8, 128), -1, I32)
    ints[me, 0:1, 0:SLOTS] = child_ref[...]
    ints[me, 1:2, 0:8] = block_ref[...]
    small[2].wait()
    for k in range(4):
        wp4[k * 64 : (k + 1) * 64, k * 128 : (k + 1) * 128] = wp_ref[...]

    int_copies, ag_sent, fw_copies = [], [], []

    def piece(ga, blk):
        first, _, sent = BLOCKS[blk]
        return gathered.at[pl.ds(pl.multiple_of(ga * 128 + first, 16), sent)]

    def forward(ga, blk, k):
        c = remote(
            piece(ga, blk), piece(ga, blk), fw_send.at[blk, k], fw_recv.at[blk, k], row, partner
        )
        c.start()
        fw_copies.append(c)

    def send(ga, blk, k, to):
        c = remote(
            piece(ga, blk), piece(ga, blk), ag_send.at[blk, k], ag_recv.at[blk, k], row, to
        )
        c.start()
        ag_sent.append(c)

    right, left, far = chip_peer(1), chip_peer(3), chip_peer(2)
    relays = {0: (0, right), 1: (1, left), 2: (0, right), 3: (1, left), 4: (0, right)}
    origin = (left, right, far)

    def arrived(blk, k):
        ga = origin[k]
        remote(
            piece(me, blk), piece(ga, blk), ag_send.at[blk, k], ag_recv.at[blk, k], row, partner
        ).wait_recv()
        if blk in relays and relays[blk][0] == k:
            send(ga, blk, 2, relays[blk][1])
        forward(ga, blk, 1 + k)

    for blk, (first, n, sent) in enumerate(BLOCKS):
        x_copies[blk].wait()
        x = x_ref[first : first + n].reshape(n * 64, 512)
        pooled = nt(p8[...], x).astype(BF)
        pooled = jnp.concatenate(
            [pooled[:, g * 256 : (g + 1) * 256] for g in range(n // 4)], axis=0
        )
        h4 = jnp.maximum(mm(pooled, wp4[...]), 0.0).astype(BF)
        for t in range(n):
            h = h4[t // 4 * 64 : t // 4 * 64 + 64, t % 4 * 128 : t % 4 * 128 + 128]
            hid_ref[pl.ds((first + t) * 64, 64), :] = h
            pp[pl.ds(t * 8, 8), :] = jnp.sum(h.astype(F32).reshape(8, 8, 128), axis=0) * 0.125
        if n < sent:
            pp[pl.ds(n * 8, (sent - n) * 8), :] = jnp.zeros(((sent - n) * 8, 128), F32)
        start = pl.multiple_of(me * 128 + first, 16)
        for w in range(8):
            gathered[pl.ds(start, sent), w * 128 : (w + 1) * 128] = pp[
                pl.ds(w, sent, stride=8), :
            ].astype(BF)
        if blk == 0:
            sides = (row > 0).astype(I32) + (row < last).astype(I32)
            pl.semaphore_wait(barrier, 7 + sides)
        if blk not in relays:
            send(me, blk, 2, far)
        send(me, blk, 0, right)
        send(me, blk, 1, left)
        forward(me, blk, 0)
        if blk == 0:
            for k in range(1, 8):
                c = remote(ints.at[me], ints.at[me], int_send.at[k], int_recv.at[k], row, peer(k))
                c.start()
                int_copies.append(c)
        if blk == 4:
            arrived(0, relays[0][0])

    for c in small[3:]:
        c.wait()
    weff[...] = nt(wc_ref[...], win_ref[...]).astype(BF)

    for c in int_copies:
        c.wait()
    child = jnp.concatenate([ints[m, 0:1, :] for m in range(8)], axis=0)
    parent = child >> 3
    block = jnp.zeros((8, 128), I32)
    for m in range(8):
        blocks = ints[m, 1:2, :]
        for i in range(8):
            block = jnp.where(parent == 8 * m + i, blocks[:, i : i + 1], block)
    octant = child & 7
    pos = (
        (octant >> 2) * 256
        + (2 * (block >> 3) + ((octant >> 1) & 1)) * 16
        + 2 * (block & 7)
        + (octant & 1)
    )
    pos = jnp.where(child >= 0, pos, -1)

    for m in range(8):
        hot = iota((512, 128), 0) == pos[m : m + 1, :]
        place[:, m * 128 : (m + 1) * 128] = jnp.where(hot, 1.0, 0.0).astype(BF)
    order = [(b, k) for b in range(NB) for k in (0, 1)]
    order += [(b, 2) for b in range(NB)]
    for blk, k in order:
        if (blk, k) != (0, relays[0][0]):
            arrived(blk, k)
    for c in fw_copies:
        c.wait_recv()

    def put(half, i):
        r = pl.ds(half * 256, 256)
        c = slice(i * 512, (i + 1) * 512)
        slab[r, c] = mm(place[r, :], gathered[:, c]).astype(BF)

    low = remote(
        halo_out.at[0],
        halo.at[1],
        halo_send.at[0],
        halo_recv.at[1],
        jnp.maximum(row - 1, 0),
        me,
    )
    high = remote(
        halo_out.at[1],
        halo.at[0],
        halo_send.at[1],
        halo_recv.at[0],
        jnp.minimum(row + 1, last),
        me,
    )

    spot = iota((32, 256), 1)
    oy, ox = spot >> 4, spot & 15
    bias = jnp.sum(
        jnp.where(iota((32, 32), 0) == iota((32, 32), 1), bias_ref[...], 0.0),
        axis=1,
        keepdims=True,
    )

    def plane(zz, ab):
        c = ((zz & 1) * 4 + ab) * 128
        return slab[pl.ds((zz >> 1) * 256, 256), c : c + 128]

    def weights(lo, hi):
        return jnp.concatenate([weff[d * 288 : (d + 1) * 288] for d in range(lo, hi)], axis=1)

    def matmuls(z):
        if z == 4:
            ds, zs = (2, 3), [0]
        elif z == 5:
            ds, zs = (0, 1), [3]
        else:
            ds = (max(0, 1 - z), min(3, 5 - z))
            zs = [z - 1 + d for d in range(*ds)]
        for a in range(2):
            x = [
                jnp.concatenate([plane(zz, 2 * a + b) for zz in zs], axis=1) for b in range(2)
            ]
            r = nt(weights(*ds), jnp.concatenate(x, axis=0))
            taps[z, 2 * a] = r[:, :256]
            taps[z, 2 * a + 1] = r[:, 256:]

    def combine(z):
        def tap(a, b, dy, dx):
            t = ((dy + 1) * 3 + dx + 1) * 32
            return taps[z, 2 * a + b, t : t + 32, :]

        for iy in range(2):
            for ix in range(2):
                ys = [(iy, 0), (1 - iy, 1 - 2 * iy)]
                xs = [(ix, 0), (1 - ix, 1 - 2 * ix)]
                ysh = (1 - iy, 2 * iy - 1)
                xsh = (1 - ix, 2 * ix - 1)
                plain = sum(tap(a, b, dy, dx) for a, dy in ys for b, dx in xs)
                only_x = sum(tap(a, xsh[0], dy, xsh[1]) for a, dy in ys)
                only_y = sum(tap(ysh[0], b, ysh[1], dx) for b, dx in xs)
                both = tap(ysh[0], xsh[0], ysh[1], xsh[1])

                def shift_x(v):
                    v = pltpu.roll(v, 255 if ix else 1, 1)
                    return jnp.where(ox == (15 if ix else 0), 0.0, v)

                def shift_y(v):
                    v = pltpu.roll(v, 240 if iy else 16, 1)
                    return jnp.where(oy == (15 if iy else 0), 0.0, v)

                total = plain + shift_x(only_x) + shift_y(only_y + shift_x(both))
                if z >= 4:
                    halo_out[z - 4, iy * 2 + ix] = total.astype(BF)
                elif z in (0, 3):
                    own[z // 3, iy * 2 + ix] = total + bias
                else:
                    finish(z, iy, ix, total + bias)

    def finish(z, iy, ix, total):
        out = jnp.maximum(total, 0.0).astype(BF)
        r = (iy * 2 + ix) * 32
        part = 0 if z in (1, 2) else 1
        rft[part, r : r + 32, (z >> 1) * 256 : ((z >> 1) + 1) * 256] = out
        r = iy * 128 + z * 32
        quad[r : r + 32, ix * 256 : (ix + 1) * 256] = out

    back_copies, own_copies = [], []

    def give_back(part):
        for i in range(2):
            m4 = mm(rft[part], place[:, i * 512 : (i + 1) * 512]).astype(BF)
            for t in range(4):
                msgs[part, 4 * i + t] = m4[:, t * 128 : (t + 1) * 128]
        for k in (4, 3, 5, 2, 6, 1, 7):
            c = remote(
                msgs.at[part, peer(k)],
                back_ref.at[part, me],
                back_send.at[part, k],
                back_recv.at[part, k],
                row,
                peer(k),
            )
            c.start()
            back_copies.append(c)
        c = pltpu.make_async_copy(msgs.at[part, me], back_ref.at[part, me], own_sem.at[part])
        c.start()
        own_copies.append(c)

    @pl.when(row == 0)
    def _():
        halo[0] = jnp.zeros((4, 32, 256), BF)

    @pl.when(row == last)
    def _():
        halo[1] = jnp.zeros((4, 32, 256), BF)

    put(0, 0)
    matmuls(4)
    combine(4)

    @pl.when(row > 0)
    def _():
        low.start()

    put(1, 1)
    matmuls(5)
    combine(5)

    @pl.when(row < last)
    def _():
        high.start()

    put(0, 1)
    put(1, 0)
    matmuls(1)
    matmuls(2)
    combine(1)
    combine(2)
    give_back(0)
    matmuls(0)
    matmuls(3)
    combine(0)
    combine(3)
    p, q = iota((512, 1), 0), iota((512, 512), 1)
    spread = ((p >> 4) & 15) * 32 + 2 * (p & 15) + (p >> 8)
    perm[...] = jnp.where(q == spread, 1.0, 0.0).astype(BF)

    @pl.when(row > 0)
    def _():
        high.wait_recv()

    @pl.when(row < last)
    def _():
        low.wait_recv()

    for z in (0, 3):
        for iy in range(2):
            for ix in range(2):
                c = iy * 2 + ix
                finish(z, iy, ix, own[z // 3, c] + halo[z // 3, c].astype(F32))
    give_back(1)

    nat = mm(quad[...], perm[...])
    for iy in range(2):
        for z in range(4):
            v = nat[iy * 128 + z * 32 : iy * 128 + z * 32 + 32]
            for t in range(16):
                tile = v[:, t // 4 * 128 : t // 4 * 128 + 128]
                if t % 4:
                    tile = pltpu.roll(tile, 128 - 32 * (t % 4), 1)
                flat[pl.ds(z * 32 + 2 * t + iy, 32, stride=128), :] = tile
    for c in range(32):
        f = flat[c * 128 : (c + 1) * 128, :][:, :32].astype(BF)
        feat_ref[c] = f.reshape(4, 32, 32)

    for c in ag_sent:
        c.wait_send()
    for c in fw_copies:
        c.wait_send()

    @pl.when(row > 0)
    def _():
        low.wait_send()

    @pl.when(row < last)
    def _():
        high.wait_send()

    for c in own_copies:
        c.wait()
    for c in back_copies:
        c.wait()


def fine_kernel(
    child_ref,
    x_ref,
    hid_ref,
    back_ref,
    wd_ref,
    ws_ref,
    feat_ref,
    out_hbm,
    root_hbm,
    up,
    lifted,
    out_ref,
    out_sem,
    root_sem,
):
    root_copy = pltpu.make_async_copy(feat_ref, root_hbm, root_sem)
    root_copy.start()
    where = column_of(iota((1, 512), 1))
    line = iota((128, 512), 0)
    for k in range(2):
        up[k] = jnp.where(line == where + 64 * k, 1.0, 0.0).astype(BF)
    for i in range(8):
        rows = slice(i % 4 * 32, i % 4 * 32 + 32)
        r = jnp.concatenate([back_ref[i // 4, j, rows, :] for j in range(8)], axis=0)
        lifted[i * 128 : (i + 1) * 128, :] = tn(r, wd_ref[...])

    copies = []
    for part, (first, count) in enumerate(PARTS):
        skips = []
        for g in range(count // 4):
            dec = []
            for k in range(4):
                s = first + 4 * g + k
                child = child_ref[s]
                lift = lifted[pl.ds(s, 8, stride=128), :]
                lift = jnp.where((child >> 2) & 1 == 0, pltpu.roll(lift, 4, 0), lift)
                lift = jnp.where(child >= 0, lift, -3e38)
                h = hid_ref[pl.ds(s * 64, 64), :].astype(F32).reshape(8, 8, 128)
                dec.append(jnp.maximum(h + lift[None], 0.0).reshape(64, 128).astype(BF))
            skips.append(nt(ws_ref[...], jnp.concatenate(dec, axis=0)).astype(BF))
        skip = jnp.concatenate(skips, axis=0)
        for k in range(4):
            r = mm(skip[:, k // 2 * 128 : k // 2 * 128 + 128], up[k % 2])
            for g in range(count // 4):
                s = first + 4 * g + k
                out_ref[s] = (x_ref[s].astype(F32) + r[g * 64 : (g + 1) * 64]).astype(BF)
        span = pl.ds(first, count)
        copies.append(pltpu.make_async_copy(out_ref.at[span], out_hbm.at[span], out_sem.at[part]))
        copies[-1].start()
    for c in copies:
        c.wait()
    root_copy.wait()


def shards(
    fine_feats, fine_child, parent_block, w_parent, w_root_in, w_root, root_bias, w_down, w_skip
):
    rows = lax.axis_size("row")
    wc = w_root.transpose(2, 3, 4, 0, 1).reshape(864, 256)
    vm = pl.BlockSpec(memory_space=pltpu.VMEM)
    anym = pl.BlockSpec(memory_space=pl.ANY)
    hbm = pl.BlockSpec(memory_space=pltpu.HBM)
    dma = pltpu.SemaphoreType.DMA
    x, hidden, back, feat = pl.pallas_call(
        functools.partial(root_kernel, rows),
        name="root",
        out_shape=(
            OUT((SLOTS, 64, 512), BF),
            OUT((SLOTS * 64, 128), BF),
            OUT((2, 8, 128, 128), BF),
            OUT((32, 4, 32, 32), BF),
        ),
        in_specs=[hbm] * 7,
        out_specs=(vm, vm, vm, vm),
        scratch_shapes=[
            pltpu.VMEM((1, SLOTS), I32),
            pltpu.VMEM((1, 8), I32),
            pltpu.VMEM((64, 128), BF),
            pltpu.VMEM((128, 256), BF),
            pltpu.VMEM((864, 256), BF),
            pltpu.VMEM((1, 32), F32),
            pltpu.VMEM((64, 512), BF),
            pltpu.VMEM((256, 512), BF),
            pltpu.VMEM((256, 128), F32),
            pltpu.VMEM((8, 8, 128), I32),
            pltpu.VMEM((1024, 1024), BF),
            pltpu.VMEM((512, 1024), BF),
            pltpu.VMEM((512, 1024), BF),
            pltpu.VMEM((2, 4, 32, 256), BF),
            pltpu.VMEM((2, 4, 32, 256), BF),
            pltpu.VMEM((2, 4, 32, 256), F32),
            pltpu.VMEM((864, 128), BF),
            pltpu.VMEM((6, 4, 288, 256), F32),
            pltpu.VMEM((2, 128, 512), BF),
            pltpu.VMEM((256, 512), BF),
            pltpu.VMEM((512, 512), BF),
            pltpu.VMEM((4096, 128), F32),
            pltpu.VMEM((2, 8, 128, 128), BF),
            dma((NB,)),
            dma((6,)),
            dma((8,)),
            dma((8,)),
            dma((NB, 3)),
            dma((NB, 3)),
            dma((NB, 4)),
            dma((NB, 4)),
            dma((2,)),
            dma((2,)),
            dma((2, 8)),
            dma((2, 8)),
            dma((2,)),
        ],
        compiler_params=pltpu.CompilerParams(
            collective_id=0, has_side_effects=True, vmem_limit_bytes=ROOT_MB * 1024 * 1024
        ),
    )(
        in_hbm(fine_child.reshape(1, SLOTS)),
        in_hbm(parent_block.reshape(1, 8)),
        in_hbm(fine_feats),
        in_hbm(w_parent),
        in_hbm(w_root_in),
        in_hbm(wc),
        in_hbm(root_bias.reshape(1, 32)),
    )
    return pl.pallas_call(
        fine_kernel,
        name="fine",
        out_shape=(
            jax.ShapeDtypeStruct((SLOTS, 64, 512), BF),
            jax.ShapeDtypeStruct((32, 4, 32, 32), BF),
        ),
        in_specs=[pl.BlockSpec(memory_space=pltpu.SMEM), vm, vm, vm, vm, vm, anym],
        out_specs=(hbm, hbm),
        scratch_shapes=[
            pltpu.VMEM((2, 128, 512), BF),
            pltpu.VMEM((1024, 128), F32),
            pltpu.VMEM((SLOTS, 64, 512), BF),
            dma((len(PARTS),)),
            dma,
        ],
        compiler_params=pltpu.CompilerParams(vmem_limit_bytes=FINE_MB * 1024 * 1024),
    )(fine_child, x, hidden, back, w_down, w_skip.T, feat)


def solution(mesh):
    return jax.shard_map(
        shards,
        mesh=mesh,
        in_specs=(
            P(("row", "ga"), None, None),
            P(("row", "ga")),
            P(("row", "ga")),
            P(),
            P(),
            P("ga", None, None, None, None),
            P("ga"),
            P(),
            P(),
        ),
        out_specs=(P(("row", "ga"), None, None), P("ga", "row", None, None)),
        check_vma=False,
    )
```

```python
import functools

import jax
import jax.numpy as jnp
from jax import lax
from jax.experimental import pallas as pl
from jax.experimental.pallas import tpu as pltpu
from jax.sharding import PartitionSpec as P

BF = jnp.bfloat16
F32 = jnp.float32
I32 = jnp.int32
MESH = pl.DeviceIdType.MESH
SLOTS = 120
BLOCKS = ((0, 16, 16), (16, 32, 32), (48, 32, 32), (80, 32, 32), (112, 8, 16))
NB = len(BLOCKS)
PARTS = ((0, 8),) + tuple((8 + 16 * i, 16) for i in range(7))
OUT = jax.ShapeDtypeStruct
ROOT_MB = 40
FINE_MB = 24


def in_hbm(a):
    return pltpu.with_memory_space_constraint(a, pltpu.HBM)


def iota(shape, dim):
    return lax.broadcasted_iota(I32, shape, dim)


def column_of(v):
    z, y, x = v >> 6, (v >> 3) & 7, v & 7
    w = (z >> 2) * 4 + (y >> 2) * 2 + (x >> 2)
    g = ((z >> 1) & 1) * 4 + ((y >> 1) & 1) * 2 + ((x >> 1) & 1)
    return g * 8 + w


def nt(a, b):
    return lax.dot_general(a, b, (((1,), (1,)), ((), ())), preferred_element_type=F32)


def tn(a, b):
    return lax.dot_general(a, b, (((0,), (0,)), ((), ())), preferred_element_type=F32)


def mm(a, b):
    return jnp.dot(a, b, preferred_element_type=F32)


def root_kernel(
    rows,
    child_hbm,
    block_hbm,
    x_hbm,
    wp_hbm,
    win_hbm,
    wc_hbm,
    bias_hbm,
    x_ref,
    hid_ref,
    back_ref,
    feat_ref,
    child_ref,
    block_ref,
    wp_ref,
    win_ref,
    wc_ref,
    bias_ref,
    p8,
    wp4,
    pp,
    ints,
    gathered,
    place,
    slab,
    halo,
    halo_out,
    own,
    weff,
    taps,
    rft,
    quad,
    perm,
    flat,
    msgs,
    x_sem,
    w_sem,
    int_send,
    int_recv,
    ag_send,
    ag_recv,
    fw_send,
    fw_recv,
    halo_send,
    halo_recv,
    back_send,
    back_recv,
    own_sem,
):
    row = lax.axis_index("row")
    me = lax.axis_index("ga")
    chip = me // 2
    core = lax.rem(me, 2)
    partner = 2 * chip + 1 - core
    last = rows - 1

    def peer(k):
        return lax.rem(me + k, 8)

    def chip_peer(k):
        return 2 * lax.rem(chip + k, 4) + core

    def remote(src, dst, send, recv, row_at, ga):
        return pltpu.make_async_remote_copy(
            src, dst, send, recv, device_id=(row_at, ga), device_id_type=MESH
        )

    x_copies = []
    for blk, (first, n, _) in enumerate(BLOCKS):
        part = pl.ds(first, n)
        x_copies.append(pltpu.make_async_copy(x_hbm.at[part], x_ref.at[part], x_sem.at[blk]))
        x_copies[-1].start()

    pairs = [
        (child_hbm, child_ref),
        (block_hbm, block_ref),
        (wp_hbm, wp_ref),
        (win_hbm, win_ref),
        (wc_hbm, wc_ref),
        (bias_hbm, bias_ref),
    ]
    small = [pltpu.make_async_copy(p, q, w_sem.at[i]) for i, (p, q) in enumerate(pairs)]
    for c in small:
        c.start()

    barrier = pltpu.get_barrier_semaphore()
    for k in range(1, 8):
        pl.semaphore_signal(barrier, inc=1, device_id=(row, peer(k)), device_id_type=MESH)

    @pl.when(row > 0)
    def _():
        pl.semaphore_signal(barrier, inc=1, device_id=(row - 1, me), device_id_type=MESH)

    @pl.when(row < last)
    def _():
        pl.semaphore_signal(barrier, inc=1, device_id=(row + 1, me), device_id_type=MESH)

    hot = column_of(iota((1, 512), 1)) == iota((64, 512), 0)
    p8[...] = jnp.where(hot, 0.125, 0.0).astype(BF)
    wp4[...] = jnp.zeros((256, 512), BF)
    small[0].wait()
    small[1].wait()
    ints[me] = jnp.full((8, 128), -1, I32)
    ints[me, 0:1, 0:SLOTS] = child_ref[...]
    ints[me, 1:2, 0:8] = block_ref[...]
    small[2].wait()
    for k in range(4):
        wp4[k * 64 : (k + 1) * 64, k * 128 : (k + 1) * 128] = wp_ref[...]

    int_copies, ag_sent, fw_copies = [], [], []

    def piece(ga, blk):
        first, _, sent = BLOCKS[blk]
        return gathered.at[pl.ds(pl.multiple_of(ga * 128 + first, 16), sent)]

    def forward(ga, blk, k):
        c = remote(
            piece(ga, blk), piece(ga, blk), fw_send.at[blk, k], fw_recv.at[blk, k], row, partner
        )
        c.start()
        fw_copies.append(c)

    def send(ga, blk, k, to):
        c = remote(
            piece(ga, blk), piece(ga, blk), ag_send.at[blk, k], ag_recv.at[blk, k], row, to
        )
        c.start()
        ag_sent.append(c)

    right, left, far = chip_peer(1), chip_peer(3), chip_peer(2)
    relays = {0: (0, right), 1: (1, left), 2: (0, right), 3: (1, left), 4: (0, right)}
    origin = (left, right, far)

    def arrived(blk, k):
        ga = origin[k]
        remote(
            piece(me, blk), piece(ga, blk), ag_send.at[blk, k], ag_recv.at[blk, k], row, partner
        ).wait_recv()
        if blk in relays and relays[blk][0] == k:
            send(ga, blk, 2, relays[blk][1])
        forward(ga, blk, 1 + k)

    for blk, (first, n, sent) in enumerate(BLOCKS):
        x_copies[blk].wait()
        x = x_ref[first : first + n].reshape(n * 64, 512)
        pooled = nt(p8[...], x).astype(BF)
        pooled = jnp.concatenate(
            [pooled[:, g * 256 : (g + 1) * 256] for g in range(n // 4)], axis=0
        )
        h4 = jnp.maximum(mm(pooled, wp4[...]), 0.0).astype(BF)
        for t in range(n):
            h = h4[t // 4 * 64 : t // 4 * 64 + 64, t % 4 * 128 : t % 4 * 128 + 128]
            hid_ref[pl.ds((first + t) * 64, 64), :] = h
            pp[pl.ds(t * 8, 8), :] = jnp.sum(h.astype(F32).reshape(8, 8, 128), axis=0) * 0.125
        if n < sent:
            pp[pl.ds(n * 8, (sent - n) * 8), :] = jnp.zeros(((sent - n) * 8, 128), F32)
        start = pl.multiple_of(me * 128 + first, 16)
        for w in range(8):
            gathered[pl.ds(start, sent), w * 128 : (w + 1) * 128] = pp[
                pl.ds(w, sent, stride=8), :
            ].astype(BF)
        if blk == 0:
            sides = (row > 0).astype(I32) + (row < last).astype(I32)
            pl.semaphore_wait(barrier, 7 + sides)
        if blk not in relays:
            send(me, blk, 2, far)
        send(me, blk, 0, right)
        send(me, blk, 1, left)
        forward(me, blk, 0)
        if blk == 0:
            for k in range(1, 8):
                c = remote(ints.at[me], ints.at[me], int_send.at[k], int_recv.at[k], row, peer(k))
                c.start()
                int_copies.append(c)
        if blk == 4:
            arrived(0, relays[0][0])

    for c in small[3:]:
        c.wait()
    weff[...] = nt(wc_ref[...], win_ref[...]).astype(BF)

    for c in int_copies:
        c.wait()
    child = jnp.concatenate([ints[m, 0:1, :] for m in range(8)], axis=0)
    parent = child >> 3
    block = jnp.zeros((8, 128), I32)
    for m in range(8):
        blocks = ints[m, 1:2, :]
        for i in range(8):
            block = jnp.where(parent == 8 * m + i, blocks[:, i : i + 1], block)
    octant = child & 7
    pos = (
        (octant >> 2) * 256
        + (2 * (block >> 3) + ((octant >> 1) & 1)) * 16
        + 2 * (block & 7)
        + (octant & 1)
    )
    pos = jnp.where(child >= 0, pos, -1)

    for m in range(8):
        hot = iota((512, 128), 0) == pos[m : m + 1, :]
        place[:, m * 128 : (m + 1) * 128] = jnp.where(hot, 1.0, 0.0).astype(BF)
    order = [(b, k) for b in range(NB) for k in (0, 1)]
    order += [(b, 2) for b in range(NB)]
    for blk, k in order:
        if (blk, k) != (0, relays[0][0]):
            arrived(blk, k)
    for c in fw_copies:
        c.wait_recv()

    def put(half, i):
        r = pl.ds(half * 256, 256)
        c = slice(i * 512, (i + 1) * 512)
        slab[r, c] = mm(place[r, :], gathered[:, c]).astype(BF)

    low = remote(
        halo_out.at[0],
        halo.at[1],
        halo_send.at[0],
        halo_recv.at[1],
        jnp.maximum(row - 1, 0),
        me,
    )
    high = remote(
        halo_out.at[1],
        halo.at[0],
        halo_send.at[1],
        halo_recv.at[0],
        jnp.minimum(row + 1, last),
        me,
    )

    spot = iota((32, 256), 1)
    oy, ox = spot >> 4, spot & 15
    bias = jnp.sum(
        jnp.where(iota((32, 32), 0) == iota((32, 32), 1), bias_ref[...], 0.0),
        axis=1,
        keepdims=True,
    )

    def plane(zz, ab):
        c = ((zz & 1) * 4 + ab) * 128
        return slab[pl.ds((zz >> 1) * 256, 256), c : c + 128]

    def weights(lo, hi):
        return jnp.concatenate([weff[d * 288 : (d + 1) * 288] for d in range(lo, hi)], axis=1)

    def matmuls(z):
        if z == 4:
            ds, zs = (2, 3), [0]
        elif z == 5:
            ds, zs = (0, 1), [3]
        else:
            ds = (max(0, 1 - z), min(3, 5 - z))
            zs = [z - 1 + d for d in range(*ds)]
        for a in range(2):
            x = [
                jnp.concatenate([plane(zz, 2 * a + b) for zz in zs], axis=1) for b in range(2)
            ]
            r = nt(weights(*ds), jnp.concatenate(x, axis=0))
            taps[z, 2 * a] = r[:, :256]
            taps[z, 2 * a + 1] = r[:, 256:]

    def combine(z):
        def tap(a, b, dy, dx):
            t = ((dy + 1) * 3 + dx + 1) * 32
            return taps[z, 2 * a + b, t : t + 32, :]

        for iy in range(2):
            for ix in range(2):
                ys = [(iy, 0), (1 - iy, 1 - 2 * iy)]
                xs = [(ix, 0), (1 - ix, 1 - 2 * ix)]
                ysh = (1 - iy, 2 * iy - 1)
                xsh = (1 - ix, 2 * ix - 1)
                plain = sum(tap(a, b, dy, dx) for a, dy in ys for b, dx in xs)
                only_x = sum(tap(a, xsh[0], dy, xsh[1]) for a, dy in ys)
                only_y = sum(tap(ysh[0], b, ysh[1], dx) for b, dx in xs)
                both = tap(ysh[0], xsh[0], ysh[1], xsh[1])

                def shift_x(v):
                    v = pltpu.roll(v, 255 if ix else 1, 1)
                    return jnp.where(ox == (15 if ix else 0), 0.0, v)

                def shift_y(v):
                    v = pltpu.roll(v, 240 if iy else 16, 1)
                    return jnp.where(oy == (15 if iy else 0), 0.0, v)

                total = plain + shift_x(only_x) + shift_y(only_y + shift_x(both))
                if z >= 4:
                    halo_out[z - 4, iy * 2 + ix] = total.astype(BF)
                elif z in (0, 3):
                    own[z // 3, iy * 2 + ix] = total + bias
                else:
                    finish(z, iy, ix, total + bias)

    def finish(z, iy, ix, total):
        out = jnp.maximum(total, 0.0).astype(BF)
        r = (iy * 2 + ix) * 32
        part = 0 if z in (1, 2) else 1
        rft[part, r : r + 32, (z >> 1) * 256 : ((z >> 1) + 1) * 256] = out
        r = iy * 128 + z * 32
        quad[r : r + 32, ix * 256 : (ix + 1) * 256] = out

    back_copies, own_copies = [], []

    def give_back(part):
        for i in range(2):
            m4 = mm(rft[part], place[:, i * 512 : (i + 1) * 512]).astype(BF)
            for t in range(4):
                msgs[part, 4 * i + t] = m4[:, t * 128 : (t + 1) * 128]
        for k in (4, 3, 5, 2, 6, 1, 7):
            c = remote(
                msgs.at[part, peer(k)],
                back_ref.at[part, me],
                back_send.at[part, k],
                back_recv.at[part, k],
                row,
                peer(k),
            )
            c.start()
            back_copies.append(c)
        c = pltpu.make_async_copy(msgs.at[part, me], back_ref.at[part, me], own_sem.at[part])
        c.start()
        own_copies.append(c)

    @pl.when(row == 0)
    def _():
        halo[0] = jnp.zeros((4, 32, 256), BF)

    @pl.when(row == last)
    def _():
        halo[1] = jnp.zeros((4, 32, 256), BF)

    put(0, 0)
    put(1, 1)
    matmuls(4)
    matmuls(5)
    combine(4)
    combine(5)

    @pl.when(row > 0)
    def _():
        low.start()

    @pl.when(row < last)
    def _():
        high.start()

    put(0, 1)
    put(1, 0)
    matmuls(1)
    matmuls(2)
    combine(1)
    combine(2)
    give_back(0)
    matmuls(0)
    matmuls(3)
    combine(0)
    combine(3)
    p, q = iota((512, 1), 0), iota((512, 512), 1)
    spread = ((p >> 4) & 15) * 32 + 2 * (p & 15) + (p >> 8)
    perm[...] = jnp.where(q == spread, 1.0, 0.0).astype(BF)

    @pl.when(row > 0)
    def _():
        high.wait_recv()

    @pl.when(row < last)
    def _():
        low.wait_recv()

    for z in (0, 3):
        for iy in range(2):
            for ix in range(2):
                c = iy * 2 + ix
                finish(z, iy, ix, own[z // 3, c] + halo[z // 3, c].astype(F32))
    give_back(1)

    nat = mm(quad[...], perm[...])
    for iy in range(2):
        for z in range(4):
            v = nat[iy * 128 + z * 32 : iy * 128 + z * 32 + 32]
            for t in range(16):
                tile = v[:, t // 4 * 128 : t // 4 * 128 + 128]
                if t % 4:
                    tile = pltpu.roll(tile, 128 - 32 * (t % 4), 1)
                flat[pl.ds(z * 32 + 2 * t + iy, 32, stride=128), :] = tile
    for c in range(32):
        f = flat[c * 128 : (c + 1) * 128, :][:, :32].astype(BF)
        feat_ref[c] = f.reshape(4, 32, 32)

    for c in ag_sent:
        c.wait_send()
    for c in fw_copies:
        c.wait_send()

    @pl.when(row > 0)
    def _():
        low.wait_send()

    @pl.when(row < last)
    def _():
        high.wait_send()

    for c in own_copies:
        c.wait()
    for c in back_copies:
        c.wait()


def fine_kernel(
    child_ref,
    x_ref,
    hid_ref,
    back_ref,
    wd_ref,
    ws_ref,
    feat_ref,
    out_hbm,
    root_hbm,
    up,
    lifted,
    out_ref,
    out_sem,
    root_sem,
):
    root_copy = pltpu.make_async_copy(feat_ref, root_hbm, root_sem)
    root_copy.start()
    where = column_of(iota((1, 512), 1))
    line = iota((128, 512), 0)
    for k in range(2):
        up[k] = jnp.where(line == where + 64 * k, 1.0, 0.0).astype(BF)
    for i in range(8):
        rows = slice(i % 4 * 32, i % 4 * 32 + 32)
        r = jnp.concatenate([back_ref[i // 4, j, rows, :] for j in range(8)], axis=0)
        lifted[i * 128 : (i + 1) * 128, :] = tn(r, wd_ref[...])

    copies = []
    for part, (first, count) in enumerate(PARTS):
        skips = []
        for g in range(count // 4):
            dec = []
            for k in range(4):
                s = first + 4 * g + k
                child = child_ref[s]
                lift = lifted[pl.ds(s, 8, stride=128), :]
                lift = jnp.where((child >> 2) & 1 == 0, pltpu.roll(lift, 4, 0), lift)
                lift = jnp.where(child >= 0, lift, -3e38)
                h = hid_ref[pl.ds(s * 64, 64), :].astype(F32).reshape(8, 8, 128)
                dec.append(jnp.maximum(h + lift[None], 0.0).reshape(64, 128).astype(BF))
            skips.append(nt(ws_ref[...], jnp.concatenate(dec, axis=0)).astype(BF))
        skip = jnp.concatenate(skips, axis=0)
        for k in range(4):
            r = mm(skip[:, k // 2 * 128 : k // 2 * 128 + 128], up[k % 2])
            for g in range(count // 4):
                s = first + 4 * g + k
                out_ref[s] = (x_ref[s].astype(F32) + r[g * 64 : (g + 1) * 64]).astype(BF)
        span = pl.ds(first, count)
        copies.append(pltpu.make_async_copy(out_ref.at[span], out_hbm.at[span], out_sem.at[part]))
        copies[-1].start()
    for c in copies:
        c.wait()
    root_copy.wait()


def shards(
    fine_feats, fine_child, parent_block, w_parent, w_root_in, w_root, root_bias, w_down, w_skip
):
    rows = lax.axis_size("row")
    wc = w_root.transpose(2, 3, 4, 0, 1).reshape(864, 256)
    vm = pl.BlockSpec(memory_space=pltpu.VMEM)
    anym = pl.BlockSpec(memory_space=pl.ANY)
    hbm = pl.BlockSpec(memory_space=pltpu.HBM)
    dma = pltpu.SemaphoreType.DMA
    x, hidden, back, feat = pl.pallas_call(
        functools.partial(root_kernel, rows),
        name="root",
        out_shape=(
            OUT((SLOTS, 64, 512), BF),
            OUT((SLOTS * 64, 128), BF),
            OUT((2, 8, 128, 128), BF),
            OUT((32, 4, 32, 32), BF),
        ),
        in_specs=[hbm] * 7,
        out_specs=(vm, vm, vm, vm),
        scratch_shapes=[
            pltpu.VMEM((1, SLOTS), I32),
            pltpu.VMEM((1, 8), I32),
            pltpu.VMEM((64, 128), BF),
            pltpu.VMEM((128, 256), BF),
            pltpu.VMEM((864, 256), BF),
            pltpu.VMEM((1, 32), F32),
            pltpu.VMEM((64, 512), BF),
            pltpu.VMEM((256, 512), BF),
            pltpu.VMEM((256, 128), F32),
            pltpu.VMEM((8, 8, 128), I32),
            pltpu.VMEM((1024, 1024), BF),
            pltpu.VMEM((512, 1024), BF),
            pltpu.VMEM((512, 1024), BF),
            pltpu.VMEM((2, 4, 32, 256), BF),
            pltpu.VMEM((2, 4, 32, 256), BF),
            pltpu.VMEM((2, 4, 32, 256), F32),
            pltpu.VMEM((864, 128), BF),
            pltpu.VMEM((6, 4, 288, 256), F32),
            pltpu.VMEM((2, 128, 512), BF),
            pltpu.VMEM((256, 512), BF),
            pltpu.VMEM((512, 512), BF),
            pltpu.VMEM((4096, 128), F32),
            pltpu.VMEM((2, 8, 128, 128), BF),
            dma((NB,)),
            dma((6,)),
            dma((8,)),
            dma((8,)),
            dma((NB, 3)),
            dma((NB, 3)),
            dma((NB, 4)),
            dma((NB, 4)),
            dma((2,)),
            dma((2,)),
            dma((2, 8)),
            dma((2, 8)),
            dma((2,)),
        ],
        compiler_params=pltpu.CompilerParams(
            collective_id=0, has_side_effects=True, vmem_limit_bytes=ROOT_MB * 1024 * 1024
        ),
    )(
        in_hbm(fine_child.reshape(1, SLOTS)),
        in_hbm(parent_block.reshape(1, 8)),
        in_hbm(fine_feats),
        in_hbm(w_parent),
        in_hbm(w_root_in),
        in_hbm(wc),
        in_hbm(root_bias.reshape(1, 32)),
    )
    return pl.pallas_call(
        fine_kernel,
        name="fine",
        out_shape=(
            jax.ShapeDtypeStruct((SLOTS, 64, 512), BF),
            jax.ShapeDtypeStruct((32, 4, 32, 32), BF),
        ),
        in_specs=[pl.BlockSpec(memory_space=pltpu.SMEM), vm, vm, vm, vm, vm, anym],
        out_specs=(hbm, hbm),
        scratch_shapes=[
            pltpu.VMEM((2, 128, 512), BF),
            pltpu.VMEM((1024, 128), F32),
            pltpu.VMEM((SLOTS, 64, 512), BF),
            dma((len(PARTS),)),
            dma,
        ],
        compiler_params=pltpu.CompilerParams(vmem_limit_bytes=FINE_MB * 1024 * 1024),
    )(fine_child, x, hidden, back, w_down, w_skip.T, feat)


def solution(mesh):
    return jax.shard_map(
        shards,
        mesh=mesh,
        in_specs=(
            P(("row", "ga"), None, None),
            P(("row", "ga")),
            P(("row", "ga")),
            P(),
            P(),
            P("ga", None, None, None, None),
            P("ga"),
            P(),
            P(),
        ),
        out_specs=(P(("row", "ga"), None, None), P("ga", "row", None, None)),
        check_vma=False,
    )
```

```python
import functools

import jax
import jax.numpy as jnp
from jax import lax
from jax.experimental import pallas as pl
from jax.experimental.pallas import tpu as pltpu
from jax.sharding import PartitionSpec as P

BF = jnp.bfloat16
F32 = jnp.float32
I32 = jnp.int32
MESH = pl.DeviceIdType.MESH
SLOTS = 120
BLOCKS = ((0, 16, 16), (16, 32, 32), (48, 32, 32), (80, 16, 16), (96, 16, 16), (112, 8, 16))
NB = len(BLOCKS)
PARTS = ((0, 8),) + tuple((8 + 16 * i, 16) for i in range(7))
OUT = jax.ShapeDtypeStruct
ROOT_MB = 40
FINE_MB = 24


def in_hbm(a):
    return pltpu.with_memory_space_constraint(a, pltpu.HBM)


def iota(shape, dim):
    return lax.broadcasted_iota(I32, shape, dim)


def column_of(v):
    z, y, x = v >> 6, (v >> 3) & 7, v & 7
    w = (z >> 2) * 4 + (y >> 2) * 2 + (x >> 2)
    g = ((z >> 1) & 1) * 4 + ((y >> 1) & 1) * 2 + ((x >> 1) & 1)
    return g * 8 + w


def nt(a, b):
    return lax.dot_general(a, b, (((1,), (1,)), ((), ())), preferred_element_type=F32)


def tn(a, b):
    return lax.dot_general(a, b, (((0,), (0,)), ((), ())), preferred_element_type=F32)


def mm(a, b):
    return jnp.dot(a, b, preferred_element_type=F32)


def root_kernel(
    rows,
    child_hbm,
    block_hbm,
    x_hbm,
    wp_hbm,
    win_hbm,
    wc_hbm,
    bias_hbm,
    x_ref,
    hid_ref,
    back_ref,
    feat_ref,
    child_ref,
    block_ref,
    wp_ref,
    win_ref,
    wc_ref,
    bias_ref,
    p8,
    wp4,
    pp,
    ints,
    gathered,
    place,
    slab,
    halo,
    halo_out,
    own,
    weff,
    taps,
    rft,
    quad,
    perm,
    flat,
    msgs,
    x_sem,
    w_sem,
    int_send,
    int_recv,
    ag_send,
    ag_recv,
    fw_send,
    fw_recv,
    halo_send,
    halo_recv,
    back_send,
    back_recv,
    own_sem,
):
    row = lax.axis_index("row")
    me = lax.axis_index("ga")
    chip = me // 2
    core = lax.rem(me, 2)
    partner = 2 * chip + 1 - core
    last = rows - 1

    def peer(k):
        return lax.rem(me + k, 8)

    def chip_peer(k):
        return 2 * lax.rem(chip + k, 4) + core

    def remote(src, dst, send, recv, row_at, ga):
        return pltpu.make_async_remote_copy(
            src, dst, send, recv, device_id=(row_at, ga), device_id_type=MESH
        )

    x_copies = []
    for blk, (first, n, _) in enumerate(BLOCKS):
        part = pl.ds(first, n)
        x_copies.append(pltpu.make_async_copy(x_hbm.at[part], x_ref.at[part], x_sem.at[blk]))
        x_copies[-1].start()

    pairs = [
        (child_hbm, child_ref),
        (block_hbm, block_ref),
        (wp_hbm, wp_ref),
        (win_hbm, win_ref),
        (wc_hbm, wc_ref),
        (bias_hbm, bias_ref),
    ]
    small = [pltpu.make_async_copy(p, q, w_sem.at[i]) for i, (p, q) in enumerate(pairs)]
    for c in small:
        c.start()

    barrier = pltpu.get_barrier_semaphore()
    for k in range(1, 8):
        pl.semaphore_signal(barrier, inc=1, device_id=(row, peer(k)), device_id_type=MESH)

    @pl.when(row > 0)
    def _():
        pl.semaphore_signal(barrier, inc=1, device_id=(row - 1, me), device_id_type=MESH)

    @pl.when(row < last)
    def _():
        pl.semaphore_signal(barrier, inc=1, device_id=(row + 1, me), device_id_type=MESH)

    hot = column_of(iota((1, 512), 1)) == iota((64, 512), 0)
    p8[...] = jnp.where(hot, 0.125, 0.0).astype(BF)
    wp4[...] = jnp.zeros((256, 512), BF)
    small[0].wait()
    small[1].wait()
    ints[me] = jnp.full((8, 128), -1, I32)
    ints[me, 0:1, 0:SLOTS] = child_ref[...]
    ints[me, 1:2, 0:8] = block_ref[...]
    small[2].wait()
    for k in range(4):
        wp4[k * 64 : (k + 1) * 64, k * 128 : (k + 1) * 128] = wp_ref[...]

    int_copies, ag_sent, fw_copies = [], [], []

    def piece(ga, blk):
        first, _, sent = BLOCKS[blk]
        return gathered.at[pl.ds(pl.multiple_of(ga * 128 + first, 16), sent)]

    def forward(ga, blk, k):
        c = remote(
            piece(ga, blk), piece(ga, blk), fw_send.at[blk, k], fw_recv.at[blk, k], row, partner
        )
        c.start()
        fw_copies.append(c)

    def send(ga, blk, k, to):
        c = remote(
            piece(ga, blk), piece(ga, blk), ag_send.at[blk, k], ag_recv.at[blk, k], row, to
        )
        c.start()
        ag_sent.append(c)

    right, left, far = chip_peer(1), chip_peer(3), chip_peer(2)
    relays = {b: (b % 2, left if b % 2 else right) for b in range(NB)}
    origin = (left, right, far)

    def arrived(blk, k):
        ga = origin[k]
        remote(
            piece(me, blk), piece(ga, blk), ag_send.at[blk, k], ag_recv.at[blk, k], row, partner
        ).wait_recv()
        if blk in relays and relays[blk][0] == k:
            send(ga, blk, 2, relays[blk][1])
        forward(ga, blk, 1 + k)

    for blk, (first, n, sent) in enumerate(BLOCKS):
        x_copies[blk].wait()
        x = x_ref[first : first + n].reshape(n * 64, 512)
        pooled = nt(p8[...], x).astype(BF)
        pooled = jnp.concatenate(
            [pooled[:, g * 256 : (g + 1) * 256] for g in range(n // 4)], axis=0
        )
        h4 = jnp.maximum(mm(pooled, wp4[...]), 0.0).astype(BF)
        for t in range(n):
            h = h4[t // 4 * 64 : t // 4 * 64 + 64, t % 4 * 128 : t % 4 * 128 + 128]
            hid_ref[pl.ds((first + t) * 64, 64), :] = h
            pp[pl.ds(t * 8, 8), :] = jnp.sum(h.astype(F32).reshape(8, 8, 128), axis=0) * 0.125
        if n < sent:
            pp[pl.ds(n * 8, (sent - n) * 8), :] = jnp.zeros(((sent - n) * 8, 128), F32)
        start = pl.multiple_of(me * 128 + first, 16)
        for w in range(8):
            gathered[pl.ds(start, sent), w * 128 : (w + 1) * 128] = pp[
                pl.ds(w, sent, stride=8), :
            ].astype(BF)
        if blk == 0:
            sides = (row > 0).astype(I32) + (row < last).astype(I32)
            pl.semaphore_wait(barrier, 7 + sides)
        if blk not in relays:
            send(me, blk, 2, far)
        send(me, blk, 0, right)
        send(me, blk, 1, left)
        forward(me, blk, 0)
        if blk == 0:
            for k in range(1, 8):
                c = remote(ints.at[me], ints.at[me], int_send.at[k], int_recv.at[k], row, peer(k))
                c.start()
                int_copies.append(c)
        if blk == 4:
            arrived(0, relays[0][0])

    for c in small[3:]:
        c.wait()
    weff[...] = nt(wc_ref[...], win_ref[...]).astype(BF)

    for c in int_copies:
        c.wait()
    child = jnp.concatenate([ints[m, 0:1, :] for m in range(8)], axis=0)
    parent = child >> 3
    block = jnp.zeros((8, 128), I32)
    for m in range(8):
        blocks = ints[m, 1:2, :]
        for i in range(8):
            block = jnp.where(parent == 8 * m + i, blocks[:, i : i + 1], block)
    octant = child & 7
    pos = (
        (octant >> 2) * 256
        + (2 * (block >> 3) + ((octant >> 1) & 1)) * 16
        + 2 * (block & 7)
        + (octant & 1)
    )
    pos = jnp.where(child >= 0, pos, -1)

    for m in range(8):
        hot = iota((512, 128), 0) == pos[m : m + 1, :]
        place[:, m * 128 : (m + 1) * 128] = jnp.where(hot, 1.0, 0.0).astype(BF)
    order = [(b, k) for b in range(NB) for k in (0, 1)]
    order += [(b, 2) for b in range(NB)]
    for blk, k in order:
        if (blk, k) != (0, relays[0][0]):
            arrived(blk, k)
    for c in fw_copies:
        c.wait_recv()

    def put(half, i):
        r = pl.ds(half * 256, 256)
        c = slice(i * 512, (i + 1) * 512)
        slab[r, c] = mm(place[r, :], gathered[:, c]).astype(BF)

    low = remote(
        halo_out.at[0],
        halo.at[1],
        halo_send.at[0],
        halo_recv.at[1],
        jnp.maximum(row - 1, 0),
        me,
    )
    high = remote(
        halo_out.at[1],
        halo.at[0],
        halo_send.at[1],
        halo_recv.at[0],
        jnp.minimum(row + 1, last),
        me,
    )

    spot = iota((32, 256), 1)
    oy, ox = spot >> 4, spot & 15
    bias = jnp.sum(
        jnp.where(iota((32, 32), 0) == iota((32, 32), 1), bias_ref[...], 0.0),
        axis=1,
        keepdims=True,
    )

    def plane(zz, ab):
        c = ((zz & 1) * 4 + ab) * 128
        return slab[pl.ds((zz >> 1) * 256, 256), c : c + 128]

    def weights(lo, hi):
        return jnp.concatenate([weff[d * 288 : (d + 1) * 288] for d in range(lo, hi)], axis=1)

    def matmuls(z):
        if z == 4:
            ds, zs = (2, 3), [0]
        elif z == 5:
            ds, zs = (0, 1), [3]
        else:
            ds = (max(0, 1 - z), min(3, 5 - z))
            zs = [z - 1 + d for d in range(*ds)]
        for a in range(2):
            x = [
                jnp.concatenate([plane(zz, 2 * a + b) for zz in zs], axis=1) for b in range(2)
            ]
            r = nt(weights(*ds), jnp.concatenate(x, axis=0))
            taps[z, 2 * a] = r[:, :256]
            taps[z, 2 * a + 1] = r[:, 256:]

    def combine(z):
        def tap(a, b, dy, dx):
            t = ((dy + 1) * 3 + dx + 1) * 32
            return taps[z, 2 * a + b, t : t + 32, :]

        for iy in range(2):
            for ix in range(2):
                ys = [(iy, 0), (1 - iy, 1 - 2 * iy)]
                xs = [(ix, 0), (1 - ix, 1 - 2 * ix)]
                ysh = (1 - iy, 2 * iy - 1)
                xsh = (1 - ix, 2 * ix - 1)
                plain = sum(tap(a, b, dy, dx) for a, dy in ys for b, dx in xs)
                only_x = sum(tap(a, xsh[0], dy, xsh[1]) for a, dy in ys)
                only_y = sum(tap(ysh[0], b, ysh[1], dx) for b, dx in xs)
                both = tap(ysh[0], xsh[0], ysh[1], xsh[1])

                def shift_x(v):
                    v = pltpu.roll(v, 255 if ix else 1, 1)
                    return jnp.where(ox == (15 if ix else 0), 0.0, v)

                def shift_y(v):
                    v = pltpu.roll(v, 240 if iy else 16, 1)
                    return jnp.where(oy == (15 if iy else 0), 0.0, v)

                total = plain + shift_x(only_x) + shift_y(only_y + shift_x(both))
                if z >= 4:
                    halo_out[z - 4, iy * 2 + ix] = total.astype(BF)
                elif z in (0, 3):
                    own[z // 3, iy * 2 + ix] = total + bias
                else:
                    finish(z, iy, ix, total + bias)

    def finish(z, iy, ix, total):
        out = jnp.maximum(total, 0.0).astype(BF)
        r = (iy * 2 + ix) * 32
        part = 0 if z in (1, 2) else 1
        rft[part, r : r + 32, (z >> 1) * 256 : ((z >> 1) + 1) * 256] = out
        r = iy * 128 + z * 32
        quad[r : r + 32, ix * 256 : (ix + 1) * 256] = out

    back_copies, own_copies = [], []

    def give_back(part):
        for i in range(2):
            m4 = mm(rft[part], place[:, i * 512 : (i + 1) * 512]).astype(BF)
            for t in range(4):
                msgs[part, 4 * i + t] = m4[:, t * 128 : (t + 1) * 128]
        for k in (4, 3, 5, 2, 6, 1, 7):
            c = remote(
                msgs.at[part, peer(k)],
                back_ref.at[part, me],
                back_send.at[part, k],
                back_recv.at[part, k],
                row,
                peer(k),
            )
            c.start()
            back_copies.append(c)
        c = pltpu.make_async_copy(msgs.at[part, me], back_ref.at[part, me], own_sem.at[part])
        c.start()
        own_copies.append(c)

    @pl.when(row == 0)
    def _():
        halo[0] = jnp.zeros((4, 32, 256), BF)

    @pl.when(row == last)
    def _():
        halo[1] = jnp.zeros((4, 32, 256), BF)

    put(0, 0)
    put(1, 1)
    matmuls(4)
    matmuls(5)
    combine(4)
    combine(5)

    @pl.when(row > 0)
    def _():
        low.start()

    @pl.when(row < last)
    def _():
        high.start()

    put(0, 1)
    put(1, 0)
    matmuls(1)
    matmuls(2)
    combine(1)
    combine(2)
    give_back(0)
    matmuls(0)
    matmuls(3)
    combine(0)
    combine(3)
    p, q = iota((512, 1), 0), iota((512, 512), 1)
    spread = ((p >> 4) & 15) * 32 + 2 * (p & 15) + (p >> 8)
    perm[...] = jnp.where(q == spread, 1.0, 0.0).astype(BF)

    @pl.when(row > 0)
    def _():
        high.wait_recv()

    @pl.when(row < last)
    def _():
        low.wait_recv()

    for z in (0, 3):
        for iy in range(2):
            for ix in range(2):
                c = iy * 2 + ix
                finish(z, iy, ix, own[z // 3, c] + halo[z // 3, c].astype(F32))
    give_back(1)

    nat = mm(quad[...], perm[...])
    for iy in range(2):
        for z in range(4):
            v = nat[iy * 128 + z * 32 : iy * 128 + z * 32 + 32]
            for t in range(16):
                tile = v[:, t // 4 * 128 : t // 4 * 128 + 128]
                if t % 4:
                    tile = pltpu.roll(tile, 128 - 32 * (t % 4), 1)
                flat[pl.ds(z * 32 + 2 * t + iy, 32, stride=128), :] = tile
    for c in range(32):
        f = flat[c * 128 : (c + 1) * 128, :][:, :32].astype(BF)
        feat_ref[c] = f.reshape(4, 32, 32)

    for c in ag_sent:
        c.wait_send()
    for c in fw_copies:
        c.wait_send()

    @pl.when(row > 0)
    def _():
        low.wait_send()

    @pl.when(row < last)
    def _():
        high.wait_send()

    for c in own_copies:
        c.wait()
    for c in back_copies:
        c.wait()


def fine_kernel(
    child_ref,
    x_ref,
    hid_ref,
    back_ref,
    wd_ref,
    ws_ref,
    feat_ref,
    out_hbm,
    root_hbm,
    up,
    lifted,
    out_ref,
    out_sem,
    root_sem,
):
    root_copy = pltpu.make_async_copy(feat_ref, root_hbm, root_sem)
    root_copy.start()
    where = column_of(iota((1, 512), 1))
    line = iota((128, 512), 0)
    for k in range(2):
        up[k] = jnp.where(line == where + 64 * k, 1.0, 0.0).astype(BF)
    for i in range(8):
        rows = slice(i % 4 * 32, i % 4 * 32 + 32)
        r = jnp.concatenate([back_ref[i // 4, j, rows, :] for j in range(8)], axis=0)
        lifted[i * 128 : (i + 1) * 128, :] = tn(r, wd_ref[...])

    copies = []
    for part, (first, count) in enumerate(PARTS):
        skips = []
        for g in range(count // 4):
            dec = []
            for k in range(4):
                s = first + 4 * g + k
                child = child_ref[s]
                lift = lifted[pl.ds(s, 8, stride=128), :]
                lift = jnp.where((child >> 2) & 1 == 0, pltpu.roll(lift, 4, 0), lift)
                lift = jnp.where(child >= 0, lift, -3e38)
                h = hid_ref[pl.ds(s * 64, 64), :].astype(F32).reshape(8, 8, 128)
                dec.append(jnp.maximum(h + lift[None], 0.0).reshape(64, 128).astype(BF))
            skips.append(nt(ws_ref[...], jnp.concatenate(dec, axis=0)).astype(BF))
        skip = jnp.concatenate(skips, axis=0)
        for k in range(4):
            r = mm(skip[:, k // 2 * 128 : k // 2 * 128 + 128], up[k % 2])
            for g in range(count // 4):
                s = first + 4 * g + k
                out_ref[s] = (x_ref[s].astype(F32) + r[g * 64 : (g + 1) * 64]).astype(BF)
        span = pl.ds(first, count)
        copies.append(pltpu.make_async_copy(out_ref.at[span], out_hbm.at[span], out_sem.at[part]))
        copies[-1].start()
    for c in copies:
        c.wait()
    root_copy.wait()


def shards(
    fine_feats, fine_child, parent_block, w_parent, w_root_in, w_root, root_bias, w_down, w_skip
):
    rows = lax.axis_size("row")
    wc = w_root.transpose(2, 3, 4, 0, 1).reshape(864, 256)
    vm = pl.BlockSpec(memory_space=pltpu.VMEM)
    anym = pl.BlockSpec(memory_space=pl.ANY)
    hbm = pl.BlockSpec(memory_space=pltpu.HBM)
    dma = pltpu.SemaphoreType.DMA
    x, hidden, back, feat = pl.pallas_call(
        functools.partial(root_kernel, rows),
        name="root",
        out_shape=(
            OUT((SLOTS, 64, 512), BF),
            OUT((SLOTS * 64, 128), BF),
            OUT((2, 8, 128, 128), BF),
            OUT((32, 4, 32, 32), BF),
        ),
        in_specs=[hbm] * 7,
        out_specs=(vm, vm, vm, vm),
        scratch_shapes=[
            pltpu.VMEM((1, SLOTS), I32),
            pltpu.VMEM((1, 8), I32),
            pltpu.VMEM((64, 128), BF),
            pltpu.VMEM((128, 256), BF),
            pltpu.VMEM((864, 256), BF),
            pltpu.VMEM((1, 32), F32),
            pltpu.VMEM((64, 512), BF),
            pltpu.VMEM((256, 512), BF),
            pltpu.VMEM((256, 128), F32),
            pltpu.VMEM((8, 8, 128), I32),
            pltpu.VMEM((1024, 1024), BF),
            pltpu.VMEM((512, 1024), BF),
            pltpu.VMEM((512, 1024), BF),
            pltpu.VMEM((2, 4, 32, 256), BF),
            pltpu.VMEM((2, 4, 32, 256), BF),
            pltpu.VMEM((2, 4, 32, 256), F32),
            pltpu.VMEM((864, 128), BF),
            pltpu.VMEM((6, 4, 288, 256), F32),
            pltpu.VMEM((2, 128, 512), BF),
            pltpu.VMEM((256, 512), BF),
            pltpu.VMEM((512, 512), BF),
            pltpu.VMEM((4096, 128), F32),
            pltpu.VMEM((2, 8, 128, 128), BF),
            dma((NB,)),
            dma((6,)),
            dma((8,)),
            dma((8,)),
            dma((NB, 3)),
            dma((NB, 3)),
            dma((NB, 4)),
            dma((NB, 4)),
            dma((2,)),
            dma((2,)),
            dma((2, 8)),
            dma((2, 8)),
            dma((2,)),
        ],
        compiler_params=pltpu.CompilerParams(
            collective_id=0, has_side_effects=True, vmem_limit_bytes=ROOT_MB * 1024 * 1024
        ),
    )(
        in_hbm(fine_child.reshape(1, SLOTS)),
        in_hbm(parent_block.reshape(1, 8)),
        in_hbm(fine_feats),
        in_hbm(w_parent),
        in_hbm(w_root_in),
        in_hbm(wc),
        in_hbm(root_bias.reshape(1, 32)),
    )
    return pl.pallas_call(
        fine_kernel,
        name="fine",
        out_shape=(
            jax.ShapeDtypeStruct((SLOTS, 64, 512), BF),
            jax.ShapeDtypeStruct((32, 4, 32, 32), BF),
        ),
        in_specs=[pl.BlockSpec(memory_space=pltpu.SMEM), vm, vm, vm, vm, vm, anym],
        out_specs=(hbm, hbm),
        scratch_shapes=[
            pltpu.VMEM((2, 128, 512), BF),
            pltpu.VMEM((1024, 128), F32),
            pltpu.VMEM((SLOTS, 64, 512), BF),
            dma((len(PARTS),)),
            dma,
        ],
        compiler_params=pltpu.CompilerParams(vmem_limit_bytes=FINE_MB * 1024 * 1024),
    )(fine_child, x, hidden, back, w_down, w_skip.T, feat)


def solution(mesh):
    return jax.shard_map(
        shards,
        mesh=mesh,
        in_specs=(
            P(("row", "ga"), None, None),
            P(("row", "ga")),
            P(("row", "ga")),
            P(),
            P(),
            P("ga", None, None, None, None),
            P("ga"),
            P(),
            P(),
        ),
        out_specs=(P(("row", "ga"), None, None), P("ga", "row", None, None)),
        check_vma=False,
    )
```
